32 devices in a mesh: row: 8 (over z, y), col: 4 (over x, core).
Axes of the slice: x: 2, y: 2, z: 4, core: 2. Of those that a mesh axis runs over, the one named last changes fastest.
Arguments:
- node_latent: bfloat16 [8192, 512], P(('row', 'col')), may hold values from -6 to 6
- edge_latent: bfloat16 [65536, 512], P(('row', 'col')), may hold values from -6 to 6
- node_cotangent: bfloat16 [8192, 512], P(('row', 'col')), may hold values from -6 to 6
- edge_cotangent: bfloat16 [65536, 512], P(('row', 'col')), may hold values from -6 to 6
- w_edge_in: bfloat16 [1536, 512], replicated, may hold values from -0.15625 to 0.15625
- w_edge_out: bfloat16 [512, 512], replicated, may hold values from -0.25 to 0.25
- w_node_in: bfloat16 [1024, 512], replicated, may hold values from -0.1875 to 0.1875
- w_node_out: bfloat16 [512, 512], replicated, may hold values from -0.25 to 0.25
- sender_code: int32 [65536], P(('row', 'col')), may hold values from 0 to 767, as said below
- receiver: int32 [65536], P(('row', 'col')), may hold values from 0 to 255
- near_list: int32 [32, 4, 64], P(('row', 'col')), may hold values from 0 to 255
- far_list: int32 [32, 32, 8], P(('row', 'col')), may hold values from 0 to 255
Outputs:
- node_new: bfloat16 [8192, 512], P(('row', 'col'))
- edge_new: bfloat16 [65536, 512], P(('row', 'col'))
- grad_node: bfloat16 [8192, 512], P(('row', 'col'))
- grad_edge: bfloat16 [65536, 512], P(('row', 'col'))
- grad_edge_in: float32 [1536, 512], P(('row', 'col'))
- grad_edge_out: float32 [512, 512], P(('row', 'col'))
- grad_node_in: float32 [1024, 512], P(('row', 'col'))
- grad_node_out: float32 [512, 512], P(('row', 'col'))
The draws below stay inside these ranges and needn't reach their ends.
Inputs may be any that keep to these rules, and one draw needn't show every extreme that they name: `sender_code`: for each block d and each device p, the far codes of block d that name p use the first c of the 8 slots, 1 <= c <= 8, c drawn for each pair, and every block uses all 8 slots of some device. Every local code, every near code and every used far code is read by at least one edge of its block.
All inputs are finite; a program needn't handle non-finite values.
Results may differ from the reference program's by a relative error of at most 0.015.
Values may be sent and summed in bfloat16 or wider, within the bound.
A program may use at most 128 MiB of HBM per device.

```python
import math
import jax
import jax.numpy as jnp
from jax import lax

D = 512
NODE_DEV = 256
NEAR = 64
FAR = 8
PEERS = 32
EDGE_DEV = 2048
NODES = 8192
EDGES = 65536
N_ROW = 8
N_COL = 4


def draw_sender_code(key, part):
    codes = NODE_DEV + 4 * NEAR + PEERS * FAR
    counts = jax.random.randint(jax.random.fold_in(key, 101), (PEERS, PEERS), 1, FAR + 1).astype(jnp.int32)
    offsets = jax.random.randint(jax.random.fold_in(key, 102), (PEERS,), 0, PEERS).astype(jnp.int32)
    devices = jnp.arange(PEERS, dtype=jnp.int32)
    full_peer = (devices + offsets) % PEERS
    counts = jnp.where(devices[None, :] == full_peer[:, None], FAR, counts)
    keys = jax.random.split(jax.random.fold_in(key, 103), PEERS)

    def one_block(count_row, block_key):
        base = jnp.arange(codes, dtype=jnp.int32)
        far_pos = base - (NODE_DEV + 4 * NEAR)
        peer = jnp.clip(far_pos // FAR, 0, PEERS - 1)
        slot = far_pos % FAR
        used = (far_pos < 0) | (slot < count_row[peer])
        spare = jax.random.randint(jax.random.fold_in(block_key, 1), (codes,), 0, NODE_DEV).astype(jnp.int32)
        mapped = jnp.where(used, base, spare)
        picks = jax.random.randint(jax.random.fold_in(block_key, 2), (EDGE_DEV - codes,), 0, codes)
        joined = jnp.concatenate([mapped, mapped[picks]])
        order = jax.random.permutation(jax.random.fold_in(block_key, 3), EDGE_DEV)
        return joined[order].astype(jnp.int32)
    return jax.vmap(one_block)(counts, keys).reshape(-1)


def place_ends(drawn, rng, low, largest):
    dims = drawn.shape
    spot = [jax.random.randint(jax.random.fold_in(rng, axis), (), 0, dims[axis]) for axis in range(len(dims))]
    drawn = drawn.at[tuple(spot)].set(low)
    longest = dims.index(max(dims))
    spot[longest] = (spot[longest] + 1) % dims[longest]
    return drawn.at[tuple(spot)].set(largest)


def block_scale(key, shape, cuts, low, top_value):
    def one(axis_at, blocks):
        draws = jax.random.uniform(jax.random.fold_in(jax.random.fold_in(key, 6), axis_at), (blocks,), jnp.float32, low / len(cuts), top_value / len(cuts))
        return jnp.repeat(jnp.exp(draws), shape[axis_at] // blocks).reshape((-1,) + (1,) * (len(shape) - axis_at - 1))

    level = one(*cuts[0])
    for cut in cuts[1:]:
        level = level * one(*cut)
    return level


def noise(own_key, dims, scale, bound, shards=(), kind=jnp.bfloat16):
    values = scale * jax.random.normal(own_key, dims, jnp.float32)
    if shards:
        values = values * block_scale(own_key, dims, shards, -0.22, 0.18)
    return jnp.clip(values, -bound, bound).astype(kind)


def setup_inputs(seed: int = 0) -> dict:
    streams_of = jax.random.split(jax.random.key(seed), 13)
    return {
        "node_latent": noise(streams_of[0], (NODES, D), 1.0, 6.0, ((0, 32),)),
        "edge_latent": noise(streams_of[1], (EDGES, D), 1.0, 6.0, ((0, 32),)),
        "node_cotangent": noise(streams_of[2], (NODES, D), 1.0, 6.0, ((0, 32),)),
        "edge_cotangent": noise(streams_of[3], (EDGES, D), 1.0, 6.0, ((0, 32),)),
        "w_edge_in": noise(streams_of[4], (3 * D, D), (3 * D) ** -0.5, 0.15625),
        "w_edge_out": noise(streams_of[5], (D, D), D ** -0.5, 0.25),
        "w_node_in": noise(streams_of[6], (2 * D, D), (2 * D) ** -0.5, 0.1875),
        "w_node_out": noise(streams_of[7], (D, D), D ** -0.5, 0.25),
        "sender_code": draw_sender_code(jax.random.fold_in(streams_of[12], 71), 0),
        "receiver": place_ends(jax.random.randint(streams_of[9], (EDGES,), 0, NODE_DEV), jax.random.fold_in(streams_of[9], 1), 0, NODE_DEV - 1).astype(jnp.int32),
        "near_list": place_ends(jax.random.randint(streams_of[10], (PEERS, 4, NEAR), 0, NODE_DEV), jax.random.fold_in(streams_of[10], 1), 0, NODE_DEV - 1).astype(jnp.int32),
        "far_list": place_ends(jax.random.randint(streams_of[11], (PEERS, PEERS, FAR), 0, NODE_DEV), jax.random.fold_in(streams_of[11], 1), 0, NODE_DEV - 1).astype(jnp.int32),
    }


EPS = 1e-05

def layer_norm(value):
    mean = lax.optimization_barrier(jnp.mean(value, -1, keepdims=True))
    centred = value - mean
    recip = lax.rsqrt(lax.optimization_barrier(jnp.mean(centred * centred, -1, keepdims=True)) + EPS)
    return centred * recip

def norm_grad(value, grad):
    mean = lax.optimization_barrier(jnp.mean(value, -1, keepdims=True))
    centred = value - mean
    recip = lax.rsqrt(lax.optimization_barrier(jnp.mean(centred * centred, -1, keepdims=True)) + EPS)
    normed = centred * recip
    inner = grad - lax.optimization_barrier(jnp.mean(grad, -1, keepdims=True)) - normed * lax.optimization_barrier(jnp.mean(grad * normed, -1, keepdims=True))
    return recip * inner

def silu_grad(value):
    sigma = jax.nn.sigmoid(value)
    return sigma * (1.0 + value * (1.0 - sigma))

def plain_dot(left, right):
    return jnp.dot(left, right, preferred_element_type=jnp.float32)

def back_dot(left, weight):
    return lax.dot_general(left, weight, (((1,), (1,)), ((), ())), preferred_element_type=jnp.float32)

def cross_dot(left, right):
    return lax.dot_general(left, right, (((0,), (0,)), ((), ())), preferred_element_type=jnp.float32)

def sender_index(sender_code, near_list, far_list):
    codes = sender_code.reshape(PEERS, EDGE_DEV).astype(jnp.int32)
    device = jnp.arange(PEERS, dtype=jnp.int32)[:, None]
    grid_row = device // N_COL
    grid_col = device % N_COL
    near_pos = codes - NODE_DEV
    kind = jnp.clip(near_pos // NEAR, 0, 3).astype(jnp.int32)
    near_slot = (near_pos % NEAR).astype(jnp.int32)
    src_row = jnp.where(kind == 0, (grid_row - 1) % N_ROW, jnp.where(kind == 1, (grid_row + 1) % N_ROW, grid_row))
    src_col = jnp.where(kind == 2, (grid_col - 1) % N_COL, jnp.where(kind == 3, (grid_col + 1) % N_COL, grid_col))
    near_src = (src_row * N_COL + src_col).astype(jnp.int32)
    near_node = near_list[near_src, kind, near_slot]
    far_pos = codes - NODE_DEV - 4 * NEAR
    peer = jnp.clip(far_pos // FAR, 0, PEERS - 1).astype(jnp.int32)
    far_slot = (far_pos % FAR).astype(jnp.int32)
    far_node = far_list[peer, jnp.broadcast_to(device, codes.shape), far_slot]
    local = device * NODE_DEV + codes
    near_global = near_src * NODE_DEV + near_node
    far_global = peer * NODE_DEV + far_node
    chosen = jnp.where(codes < NODE_DEV, local, jnp.where(far_pos < 0, near_global, far_global))
    return chosen.astype(jnp.int32)

def reference(node_latent, edge_latent, node_cotangent, edge_cotangent, w_edge_in, w_edge_out, w_node_in, w_node_out, sender_code, receiver, near_list, far_list):
    width = D
    senders = sender_index(sender_code, near_list, far_list)
    local_recv = receiver.reshape(PEERS, EDGE_DEV).astype(jnp.int32)
    global_recv = (local_recv + jnp.arange(PEERS, dtype=jnp.int32)[:, None] * NODE_DEV).astype(jnp.int32)
    edge_blocks = edge_latent.reshape(PEERS, EDGE_DEV, width)
    cot_blocks = edge_cotangent.reshape(PEERS, EDGE_DEV, width)
    w_e = w_edge_in[:width]
    w_s = w_edge_in[width:2 * width]
    w_r = w_edge_in[2 * width:]
    node_ids = jnp.arange(NODE_DEV, dtype=jnp.int32)[:, None]

    def edge_front(edges, send_idx, recv_idx):
        sent_rows = jnp.take(node_latent, send_idx, axis=0)
        recv_rows = jnp.take(node_latent, recv_idx, axis=0)
        edge_pre = plain_dot(edges, w_e) + plain_dot(sent_rows, w_s) + plain_dot(recv_rows, w_r)
        edge_hidden = jax.nn.silu(edge_pre).astype(jnp.bfloat16)
        edge_mid = plain_dot(edge_hidden, w_edge_out)
        return (sent_rows, recv_rows, edge_pre, edge_hidden, edge_mid)

    def forward_block(block):
        edges, send_idx, recv_idx, recv_local = block
        parts = edge_front(edges, send_idx, recv_idx)
        edge_new = (edges.astype(jnp.float32) + layer_norm(parts[4])).astype(jnp.bfloat16)
        onehot = (recv_local[None, :] == node_ids).astype(jnp.bfloat16)
        gathered = plain_dot(onehot, edge_new).astype(jnp.bfloat16)
        return (edge_new, gathered)
    edge_new, gathered = lax.map(forward_block, (edge_blocks, senders, global_recv, local_recv))
    edge_new = edge_new.reshape(EDGES, width)
    gathered = gathered.reshape(NODES, width)
    node_pre = plain_dot(node_latent, w_node_in[:width]) + plain_dot(gathered, w_node_in[width:])
    node_hidden = jax.nn.silu(node_pre).astype(jnp.bfloat16)
    node_mid = plain_dot(node_hidden, w_node_out)
    node_new = (node_latent.astype(jnp.float32) + layer_norm(node_mid)).astype(jnp.bfloat16)
    node_delta = norm_grad(node_mid, node_cotangent.astype(jnp.float32)).astype(jnp.bfloat16)
    node_pre_delta = (back_dot(node_delta, w_node_out) * silu_grad(node_pre)).astype(jnp.bfloat16)
    gathered_grad = back_dot(node_pre_delta, w_node_in[width:])
    node_in_grad = back_dot(node_pre_delta, w_node_in[:width])
    grad_node_in = jnp.concatenate([cross_dot(node_latent, node_pre_delta), cross_dot(gathered, node_pre_delta)], 0)
    grad_node_out = cross_dot(node_hidden, node_delta)

    def backward_block(carry, block):
        node_acc, acc_in, acc_out = carry
        edges, cots, send_idx, recv_idx = block
        sent_rows, recv_rows, edge_pre, edge_hidden, edge_mid = edge_front(edges, send_idx, recv_idx)
        edge_total = cots.astype(jnp.float32) + jnp.take(gathered_grad, recv_idx, axis=0)
        edge_delta = norm_grad(edge_mid, edge_total).astype(jnp.bfloat16)
        edge_pre_delta = (back_dot(edge_delta, w_edge_out) * silu_grad(edge_pre)).astype(jnp.bfloat16)
        grad_edge = (edge_total + back_dot(edge_pre_delta, w_e)).astype(jnp.bfloat16)
        node_acc = node_acc.at[send_idx].add(back_dot(edge_pre_delta, w_s))
        node_acc = node_acc.at[recv_idx].add(back_dot(edge_pre_delta, w_r))
        block_in = jnp.concatenate([cross_dot(edges, edge_pre_delta), cross_dot(sent_rows, edge_pre_delta), cross_dot(recv_rows, edge_pre_delta)], 0)
        acc_in = acc_in + block_in
        acc_out = acc_out + cross_dot(edge_hidden, edge_delta)
        return ((node_acc, acc_in, acc_out), grad_edge)
    start = (jnp.zeros((NODES, width), jnp.float32), jnp.zeros((3 * width, width), jnp.float32), jnp.zeros((width, width), jnp.float32))
    (node_acc, acc_in, acc_out), grad_edge = lax.scan(backward_block, start, (edge_blocks, cot_blocks, senders, global_recv))
    grad_edge = grad_edge.reshape(EDGES, width)
    grad_node = (node_cotangent.astype(jnp.float32) + node_in_grad + node_acc).astype(jnp.bfloat16)
    edge_scale = 1.0 / math.sqrt(EDGES)
    node_scale = 1.0 / math.sqrt(NODES)
    return (node_new, edge_new, grad_node, grad_edge, acc_in * edge_scale, acc_out * edge_scale, grad_node_in * node_scale, grad_node_out * node_scale)
```

```python
import functools
import math

import jax
import jax.numpy as jnp
from jax import lax
from jax.experimental import pallas as pl
from jax.experimental.pallas import tpu as pltpu
from jax.sharding import PartitionSpec as P

EPS = 1e-05
MESH = pl.DeviceIdType.MESH
F32 = jnp.float32
BF16 = jnp.bfloat16


def passed_along(value, axis, by):
    peers = lax.axis_size(axis)
    return lax.ppermute(value, axis, [(i, (i + by) % peers) for i in range(peers)])


def dot(left, right):
    return jnp.dot(left, right, preferred_element_type=F32)


def dot_t(left, weight):
    return lax.dot_general(left, weight, (((1,), (1,)), ((), ())), preferred_element_type=F32)


def cross(left, right):
    return lax.dot_general(left, right, (((0,), (0,)), ((), ())), preferred_element_type=F32)


def norm_parts(value):
    mean = jnp.mean(value, -1, keepdims=True)
    centred = value - mean
    recip = lax.rsqrt(jnp.mean(centred * centred, -1, keepdims=True) + EPS)
    return centred * recip, recip


def norm_back(normed, recip, grad):
    inner = (
        grad
        - jnp.mean(grad, -1, keepdims=True)
        - normed * jnp.mean(grad * normed, -1, keepdims=True)
    )
    return recip * inner


def row_hot(codes, count):
    tile = codes.shape[1]
    column = jnp.transpose(jnp.broadcast_to(codes, (128, tile)))
    lane = lax.broadcasted_iota(jnp.int32, (tile, 128), 1)
    groups = [
        jnp.where(column == lane + 128 * g, 1.0, 0.0).astype(BF16) for g in range(count // 128)
    ]
    return jnp.concatenate(groups, 1)


def col_hot(codes, count):
    tile = codes.shape[1]
    ids = lax.broadcasted_iota(jnp.int32, (count, tile), 0)
    return jnp.where(codes == ids, 1.0, 0.0).astype(BF16)


def compute_kernel(
    tile,
    edge_scale,
    node_scale,
    node_ref,
    edge_ref,
    ncot_ref,
    ecot_ref,
    w_in,
    w_out,
    v_in,
    v_out,
    code_ref,
    recv_ref,
    ext_ref,
    node_new_ref,
    edge_new_ref,
    part_ref,
    grad_edge_ref,
    ext_grad_ref,
    g_in_ref,
    g_out_ref,
    h_in_ref,
    h_out_ref,
    proj,
    slope,
    normed_s,
    recip_s,
    hidden_s,
    gath_s,
    gg_s,
    sums_s,
    acc_e,
    acc_o,
):
    nodes, width = node_ref.shape
    edges = edge_ref.shape[0]
    ext = ext_ref.shape[0]
    rows = nodes + ext
    steps = edges // tile
    w_e = w_in.at[pl.ds(0, width)]
    w_s = w_in.at[pl.ds(width, width)]
    w_r = w_in.at[pl.ds(2 * width, width)]
    v_a = v_in.at[pl.ds(0, width)]
    v_b = v_in.at[pl.ds(width, width)]
    proj[pl.ds(0, nodes), :] = dot(node_ref[...], w_s[...]).astype(BF16)
    proj[pl.ds(nodes, ext), :] = dot(ext_ref[...], w_s[...]).astype(BF16)
    proj[pl.ds(rows, nodes), :] = dot(node_ref[...], w_r[...]).astype(BF16)
    gath_s[...] = jnp.zeros_like(gath_s)

    def forward(step, carry):
        span = pl.ds(pl.multiple_of(step * tile, tile), tile)
        codes = code_ref[step]
        recvs = recv_ref[step]
        hot = jnp.concatenate([row_hot(codes, rows), row_hot(recvs, nodes)], 1)
        edge = edge_ref[span, :]
        pre = dot(edge, w_e[...]) + dot(hot, proj[...])
        sigma = jax.nn.sigmoid(pre)
        slope[span, :] = sigma * (1.0 + pre * (1.0 - sigma))
        hidden = (pre * sigma).astype(BF16)
        hidden_s[span, :] = hidden
        normed, recip = norm_parts(dot(hidden, w_out[...]))
        normed_s[span, :] = normed
        recip_s[span, :] = jnp.broadcast_to(recip, (tile, 128))
        new = (edge.astype(F32) + normed).astype(BF16)
        edge_new_ref[span, :] = new
        gath_s[...] += dot(col_hot(recvs, nodes), new)
        return carry

    lax.fori_loop(0, steps, forward, 0)

    node = node_ref[...]
    gathered = gath_s[...].astype(BF16)
    pre = dot(node, v_a[...]) + dot(gathered, v_b[...])
    sigma = jax.nn.sigmoid(pre)
    hidden = (pre * sigma).astype(BF16)
    normed, recip = norm_parts(dot(hidden, v_out[...]))
    node_new_ref[...] = (node.astype(F32) + normed).astype(BF16)
    ncot = ncot_ref[...].astype(F32)
    delta = norm_back(normed, recip, ncot).astype(BF16)
    pre_delta = (dot_t(delta, v_out[...]) * (sigma * (1.0 + pre * (1.0 - sigma)))).astype(BF16)
    gg_s[...] = dot_t(pre_delta, v_b[...]).astype(BF16)
    part_ref[...] = ncot + dot_t(pre_delta, v_a[...])
    h_in_ref[pl.ds(0, width), :] = (cross(node, pre_delta) * node_scale).astype(BF16)
    h_in_ref[pl.ds(width, width), :] = (cross(gathered, pre_delta) * node_scale).astype(BF16)
    h_out_ref[...] = (cross(hidden, delta) * node_scale).astype(BF16)

    sums_s[...] = jnp.zeros_like(sums_s)
    acc_e[...] = jnp.zeros_like(acc_e)
    acc_o[...] = jnp.zeros_like(acc_o)

    def backward(step, carry):
        span = pl.ds(pl.multiple_of(step * tile, tile), tile)
        codes = code_ref[step]
        recvs = recv_ref[step]
        total = ecot_ref[span, :].astype(F32) + dot(row_hot(recvs, nodes), gg_s[...])
        recip = recip_s[span, :][:, :1]
        delta = norm_back(normed_s[span, :], recip, total).astype(BF16)
        pre_delta = (dot_t(delta, w_out[...]) * slope[span, :]).astype(BF16)
        grad_edge_ref[span, :] = (total + dot_t(pre_delta, w_e[...])).astype(BF16)
        hot = jnp.concatenate([col_hot(codes, rows), col_hot(recvs, nodes)], 0)
        sums_s[...] += dot(hot, pre_delta)
        acc_e[...] += cross(edge_ref[span, :], pre_delta)
        acc_o[...] += cross(hidden_s[span, :], delta)
        return carry

    lax.fori_loop(0, steps, backward, 0)

    g_in_ref[pl.ds(0, width), :] = (acc_e[...] * edge_scale).astype(BF16)
    g_out_ref[...] = (acc_o[...] * edge_scale).astype(BF16)
    near = sums_s[pl.ds(0, nodes), :].astype(BF16)
    far = sums_s[pl.ds(nodes, ext), :].astype(BF16)
    recv = sums_s[pl.ds(rows, nodes), :].astype(BF16)
    ext_grad_ref[...] = dot_t(far, w_s[...]).astype(BF16)
    part_ref[...] += dot_t(near, w_s[...]) + dot_t(recv, w_r[...])
    g_in_ref[pl.ds(width, width), :] = (
        (cross(node_ref[...], near) + cross(ext_ref[...], far)) * edge_scale
    ).astype(BF16)
    g_in_ref[pl.ds(2 * width, width), :] = (cross(node_ref[...], recv) * edge_scale).astype(BF16)


def compute(node, edge, ncot, ecot, w_in, w_out, v_in, v_out, code, recv, ext, scales):
    nodes, width = node.shape
    edges = edge.shape[0]
    rows = nodes + ext.shape[0]
    tile = math.gcd(edges, 512)
    vmem = pl.BlockSpec(memory_space=pltpu.VMEM)
    shape = jax.ShapeDtypeStruct
    units = 2 * edges * width
    work = units * width * 5 + units * (2 * (rows + nodes) + 2 * nodes)
    return pl.pallas_call(
        functools.partial(compute_kernel, tile, *scales),
        name="processor",
        out_shape=(
            shape((nodes, width), BF16),
            shape((edges, width), BF16),
            shape((nodes, width), F32),
            shape((edges, width), BF16),
            shape(ext.shape, BF16),
            shape(w_in.shape, BF16),
            shape(w_out.shape, BF16),
            shape(v_in.shape, BF16),
            shape(v_out.shape, BF16),
        ),
        in_specs=[vmem] * 11,
        out_specs=[vmem] * 9,
        scratch_shapes=[
            pltpu.VMEM((rows + nodes, width), BF16),
            pltpu.VMEM((edges, width), F32),
            pltpu.VMEM((edges, width), F32),
            pltpu.VMEM((edges, 128), F32),
            pltpu.VMEM((edges, width), BF16),
            pltpu.VMEM((nodes, width), F32),
            pltpu.VMEM((nodes, width), BF16),
            pltpu.VMEM((rows + nodes, width), F32),
            pltpu.VMEM((width, width), F32),
            pltpu.VMEM((width, width), F32),
        ],
        compiler_params=pltpu.CompilerParams(vmem_limit_bytes=62 * 1024 * 1024),
        cost_estimate=pl.CostEstimate(flops=work, bytes_accessed=20 * units, transcendentals=units),
    )(
        node,
        edge,
        ncot,
        ecot,
        w_in,
        w_out,
        v_in,
        v_out,
        code.reshape(edges // tile, 1, tile),
        recv.reshape(edges // tile, 1, tile),
        ext,
    )


def bit_count(size):
    bits = size.bit_length() - 1
    assert size == 1 << bits
    return bits


def scatter_kernel(orders, row_bits, col_bits, count, *refs):
    bits = row_bits + col_bits
    inputs = refs[:count]
    outputs = refs[count : 2 * count]
    recv = [refs[2 * count + a * bits : 2 * count + (a + 1) * bits] for a in range(count)]
    at = 2 * count + count * bits
    held = [refs[at + a * (bits - 1) : at + (a + 1) * (bits - 1)] for a in range(count)]
    send_sem, recv_sem = refs[-2:]
    row = lax.axis_index("row")
    col = lax.axis_index("col")

    def mine(bit):
        if bit < row_bits:
            return (row // (1 << (row_bits - 1 - bit))) % 2
        return (col // (1 << (bits - 1 - bit))) % 2

    def partner(bit):
        if bit < row_bits:
            step = 1 << (row_bits - 1 - bit)
            return (row + step * (1 - 2 * mine(bit)), col)
        step = 1 << (bits - 1 - bit)
        return (row, col + step * (1 - 2 * mine(bit)))

    barrier = pltpu.get_barrier_semaphore()
    for bit in range(bits):
        pl.semaphore_signal(barrier, inc=1, device_id=partner(bit), device_id_type=MESH)
    pl.semaphore_wait(barrier, bits)

    left = [list(range(bits)) for _ in range(count)]
    current = list(inputs)

    def copy_of(a, phase):
        bit = orders[a][phase]
        place = left[a].index(bit)
        spot = (slice(None),) * place + (1 - mine(bit),)
        return pltpu.make_async_remote_copy(
            src_ref=current[a].at[spot],
            dst_ref=recv[a][phase],
            send_sem=send_sem.at[a, phase],
            recv_sem=recv_sem.at[a, phase],
            device_id=partner(bit),
            device_id_type=MESH,
        )

    copies = [copy_of(a, 0) for a in range(count)]
    for item in copies:
        item.start()
    sent = []
    for phase in range(bits):
        for a in range(count):
            copies[a].wait_recv()
            sent.append(copies[a])
            bit = orders[a][phase]
            place = left[a].index(bit)
            spot = (slice(None),) * place + (mine(bit),)
            value = current[a][spot].astype(F32) + recv[a][phase][...].astype(F32)
            left[a].remove(bit)
            if phase == bits - 1:
                outputs[a][...] = value
            else:
                held[a][phase][...] = value.astype(BF16)
                current[a] = held[a][phase]
                copies[a] = copy_of(a, phase + 1)
                copies[a].start()
    for item in sent:
        item.wait_send()


def scatter_sum(grads):
    rows_grid = lax.axis_size("row")
    cols_grid = lax.axis_size("col")
    row_bits = bit_count(rows_grid)
    col_bits = bit_count(cols_grid)
    bits = row_bits + col_bits
    peers = rows_grid * cols_grid
    width = grads[0].shape[-1]
    slabs = [g.shape[0] // peers for g in grads]
    shaped = [g.reshape((2,) * bits + (s, width)) for g, s in zip(grads, slabs)]
    core = bits - 1
    along_col = list(range(bits - 2, row_bits - 1, -1))
    row_near = [row_bits - 1]
    row_far = list(range(row_bits - 2, -1, -1))
    turns = [
        [core] + along_col + row_near + row_far,
        [core] + row_near + row_far + along_col,
        [core] + row_far + along_col + row_near,
        [core] + row_far + along_col + row_near,
    ]
    count = len(grads)
    vmem = pl.BlockSpec(memory_space=pltpu.VMEM)
    recv = [
        pltpu.VMEM((2,) * (bits - 1 - phase) + (s, width), BF16)
        for s in slabs
        for phase in range(bits)
    ]
    held = [
        pltpu.VMEM((2,) * (bits - 1 - phase) + (s, width), BF16)
        for s in slabs
        for phase in range(bits - 1)
    ]
    return pl.pallas_call(
        functools.partial(scatter_kernel, turns, row_bits, col_bits, count),
        name="scatter_sum",
        out_shape=tuple(jax.ShapeDtypeStruct((s, width), F32) for s in slabs),
        in_specs=[vmem] * count,
        out_specs=[vmem] * count,
        scratch_shapes=recv
        + held
        + [pltpu.SemaphoreType.DMA((count, bits)), pltpu.SemaphoreType.DMA((count, bits))],
        compiler_params=pltpu.CompilerParams(
            collective_id=0, has_side_effects=True, vmem_limit_bytes=40 * 1024 * 1024
        ),
        cost_estimate=pl.CostEstimate(flops=10**9, bytes_accessed=10**8, transcendentals=0),
    )(*shaped)


def shards(
    node_latent,
    edge_latent,
    node_cotangent,
    edge_cotangent,
    w_edge_in,
    w_edge_out,
    w_node_in,
    w_node_out,
    sender_code,
    receiver,
    near_list,
    far_list,
):
    node_rows, width = node_latent.shape
    edge_rows = edge_latent.shape[0]
    peers = lax.axis_size("row") * lax.axis_size("col")
    near_width = near_list.shape[2]
    far_width = far_list.shape[2]
    near_rows = 4 * near_width
    moves = (("row", 1), ("row", -1), ("col", 1), ("col", -1))
    owner = jnp.concatenate([near_list.reshape(-1), far_list.reshape(-1)], 0)
    node_ids = jnp.arange(node_rows, dtype=jnp.int32)
    offered = dot((owner[:, None] == node_ids[None, :]).astype(BF16), node_latent).astype(BF16)
    parts = []
    for slot, (axis, by) in enumerate(moves):
        parts.append(
            passed_along(offered[slot * near_width : (slot + 1) * near_width], axis, by)
        )
    far_send = offered[near_rows:].reshape(peers, far_width, width)
    far_recv = lax.all_to_all(far_send, ("row", "col"), split_axis=0, concat_axis=0, tiled=True)
    ext = jnp.concatenate(parts + [far_recv.reshape(peers * far_width, width)], 0)
    scales = (1.0 / math.sqrt(edge_rows * peers), 1.0 / math.sqrt(node_rows * peers))
    node_new, edge_new, part, grad_edge, ext_grad, g_in, g_out, h_in, h_out = compute(
        node_latent,
        edge_latent,
        node_cotangent,
        edge_cotangent,
        w_edge_in,
        w_edge_out,
        w_node_in,
        w_node_out,
        sender_code,
        receiver,
        ext,
        scales,
    )
    back = []
    for slot, (axis, by) in enumerate(moves):
        back.append(
            passed_along(ext_grad[slot * near_width : (slot + 1) * near_width], axis, -by)
        )
    far_back = lax.all_to_all(
        ext_grad[near_rows:].reshape(peers, far_width, width),
        ("row", "col"),
        split_axis=0,
        concat_axis=0,
        tiled=True,
    )
    returned = jnp.concatenate(back + [far_back.reshape(peers * far_width, width)], 0)
    owner_hot = (node_ids[:, None] == owner[None, :]).astype(BF16)
    grad_node = (part + dot(owner_hot, returned)).astype(BF16)
    s_in, s_hin, s_out, s_hout = scatter_sum((g_in, h_in, g_out, h_out))
    return (node_new, edge_new, grad_node, grad_edge, s_in, s_out, s_hin, s_hout)


def solution(mesh):
    both = ("row", "col")
    in_specs = (
        P(both, None),
        P(both, None),
        P(both, None),
        P(both, None),
        P(),
        P(),
        P(),
        P(),
        P(both),
        P(both),
        P(both, None, None),
        P(both, None, None),
    )
    out_specs = (P(both, None),) * 8
    return jax.shard_map(shards, mesh=mesh, in_specs=in_specs, out_specs=out_specs, check_vma=False)
```

```python
import functools
import math

import jax
import jax.numpy as jnp
from jax import lax
from jax.experimental import pallas as pl
from jax.experimental.pallas import tpu as pltpu
from jax.sharding import PartitionSpec as P

EPS = 1e-05
MESH = pl.DeviceIdType.MESH
F32 = jnp.float32
BF16 = jnp.bfloat16


def dot(left, right):
    return jnp.dot(left, right, preferred_element_type=F32)


def dot_t(left, weight):
    return lax.dot_general(left, weight, (((1,), (1,)), ((), ())), preferred_element_type=F32)


def cross(left, right):
    return lax.dot_general(left, right, (((0,), (0,)), ((), ())), preferred_element_type=F32)


def norm_parts(value):
    mean = jnp.mean(value, -1, keepdims=True)
    centred = value - mean
    recip = lax.rsqrt(jnp.mean(centred * centred, -1, keepdims=True) + EPS)
    return centred * recip, recip


def norm_back(normed, recip, grad):
    inner = (
        grad
        - jnp.mean(grad, -1, keepdims=True)
        - normed * jnp.mean(grad * normed, -1, keepdims=True)
    )
    return recip * inner


def row_hot(codes, count):
    tile = codes.shape[1]
    column = jnp.transpose(jnp.broadcast_to(codes, (128, tile)))
    lane = lax.broadcasted_iota(jnp.int32, (tile, 128), 1)
    groups = [
        jnp.where(column == lane + 128 * g, 1.0, 0.0).astype(BF16) for g in range(count // 128)
    ]
    return jnp.concatenate(groups, 1)


def col_hot(codes, count):
    tile = codes.shape[1]
    ids = lax.broadcasted_iota(jnp.int32, (count, tile), 0)
    return jnp.where(codes == ids, 1.0, 0.0).astype(BF16)


def compute_kernel(
    tile,
    edge_scale,
    node_scale,
    node_ref,
    edge_ref,
    ncot_ref,
    ecot_ref,
    w_in,
    w_out,
    v_in,
    v_out,
    code_ref,
    recv_ref,
    near_ref,
    far_ref,
    node_new_ref,
    edge_new_ref,
    part_ref,
    grad_edge_ref,
    near_grad_ref,
    far_grad_ref,
    g_in_ref,
    g_out_ref,
    h_in_ref,
    h_out_ref,
    proj,
    slope,
    normed_s,
    recip_s,
    hidden_s,
    gath_s,
    gg_s,
    sums_s,
    acc_e,
    acc_o,
):
    nodes, width = node_ref.shape
    edges = edge_ref.shape[0]
    near = near_ref.shape[0]
    far = far_ref.shape[0]
    rows = nodes + near + far
    steps = edges // tile
    w_e = w_in.at[pl.ds(0, width)]
    w_s = w_in.at[pl.ds(width, width)]
    w_r = w_in.at[pl.ds(2 * width, width)]
    v_a = v_in.at[pl.ds(0, width)]
    v_b = v_in.at[pl.ds(width, width)]
    proj[pl.ds(0, nodes), :] = dot(node_ref[...], w_s[...]).astype(BF16)
    proj[pl.ds(nodes, near), :] = dot(near_ref[...], w_s[...]).astype(BF16)
    proj[pl.ds(nodes + near, far), :] = dot(far_ref[...], w_s[...]).astype(BF16)
    proj[pl.ds(rows, nodes), :] = dot(node_ref[...], w_r[...]).astype(BF16)
    gath_s[...] = jnp.zeros_like(gath_s)

    def forward(step, carry):
        span = pl.ds(pl.multiple_of(step * tile, tile), tile)
        codes = code_ref[step]
        recvs = recv_ref[step]
        hot = jnp.concatenate([row_hot(codes, rows), row_hot(recvs, nodes)], 1)
        edge = edge_ref[span, :]
        pre = dot(edge, w_e[...]) + dot(hot, proj[...])
        sigma = jax.nn.sigmoid(pre)
        slope[span, :] = sigma * (1.0 + pre * (1.0 - sigma))
        hidden = (pre * sigma).astype(BF16)
        hidden_s[span, :] = hidden
        normed, recip = norm_parts(dot(hidden, w_out[...]))
        normed_s[span, :] = normed
        recip_s[span, :] = jnp.broadcast_to(recip, (tile, 128))
        new = (edge.astype(F32) + normed).astype(BF16)
        edge_new_ref[span, :] = new
        gath_s[...] += dot(col_hot(recvs, nodes), new)
        return carry

    lax.fori_loop(0, steps, forward, 0)

    node = node_ref[...]
    gathered = gath_s[...].astype(BF16)
    pre = dot(node, v_a[...]) + dot(gathered, v_b[...])
    sigma = jax.nn.sigmoid(pre)
    hidden = (pre * sigma).astype(BF16)
    normed, recip = norm_parts(dot(hidden, v_out[...]))
    node_new_ref[...] = (node.astype(F32) + normed).astype(BF16)
    ncot = ncot_ref[...].astype(F32)
    delta = norm_back(normed, recip, ncot).astype(BF16)
    pre_delta = (dot_t(delta, v_out[...]) * (sigma * (1.0 + pre * (1.0 - sigma)))).astype(BF16)
    gg_s[...] = dot_t(pre_delta, v_b[...]).astype(BF16)
    part_ref[...] = ncot + dot_t(pre_delta, v_a[...])
    h_in_ref[pl.ds(0, width), :] = (cross(node, pre_delta) * node_scale).astype(BF16)
    h_in_ref[pl.ds(width, width), :] = (cross(gathered, pre_delta) * node_scale).astype(BF16)
    h_out_ref[...] = (cross(hidden, delta) * node_scale).astype(BF16)

    sums_s[...] = jnp.zeros_like(sums_s)
    acc_e[...] = jnp.zeros_like(acc_e)
    acc_o[...] = jnp.zeros_like(acc_o)

    def backward(step, carry):
        span = pl.ds(pl.multiple_of(step * tile, tile), tile)
        codes = code_ref[step]
        recvs = recv_ref[step]
        total = ecot_ref[span, :].astype(F32) + dot(row_hot(recvs, nodes), gg_s[...])
        recip = recip_s[span, :][:, :1]
        delta = norm_back(normed_s[span, :], recip, total).astype(BF16)
        pre_delta = (dot_t(delta, w_out[...]) * slope[span, :]).astype(BF16)
        grad_edge_ref[span, :] = (total + dot_t(pre_delta, w_e[...])).astype(BF16)
        hot = jnp.concatenate([col_hot(codes, rows), col_hot(recvs, nodes)], 0)
        sums_s[...] += dot(hot, pre_delta)
        acc_e[...] += cross(edge_ref[span, :], pre_delta)
        acc_o[...] += cross(hidden_s[span, :], delta)
        return carry

    lax.fori_loop(0, steps, backward, 0)

    g_in_ref[pl.ds(0, width), :] = (acc_e[...] * edge_scale).astype(BF16)
    g_out_ref[...] = (acc_o[...] * edge_scale).astype(BF16)
    own_sum = sums_s[pl.ds(0, nodes), :].astype(BF16)
    near_sum = sums_s[pl.ds(nodes, near), :].astype(BF16)
    far_sum = sums_s[pl.ds(nodes + near, far), :].astype(BF16)
    recv_sum = sums_s[pl.ds(rows, nodes), :].astype(BF16)
    near_grad_ref[...] = dot_t(near_sum, w_s[...]).astype(BF16)
    far_grad_ref[...] = dot_t(far_sum, w_s[...]).astype(BF16)
    part_ref[...] += dot_t(own_sum, w_s[...]) + dot_t(recv_sum, w_r[...])
    sent = cross(node_ref[...], own_sum) + cross(near_ref[...], near_sum)
    sent += cross(far_ref[...], far_sum)
    g_in_ref[pl.ds(width, width), :] = (sent * edge_scale).astype(BF16)
    g_in_ref[pl.ds(2 * width, width), :] = (cross(node_ref[...], recv_sum) * edge_scale).astype(BF16)


def compute(node, edge, ncot, ecot, w_in, w_out, v_in, v_out, code, recv, near, far, scales):
    nodes, width = node.shape
    edges = edge.shape[0]
    rows = nodes + near.shape[0] + far.shape[0]
    tile = math.gcd(edges, 512)
    vmem = pl.BlockSpec(memory_space=pltpu.VMEM)
    shape = jax.ShapeDtypeStruct
    units = 2 * edges * width
    work = units * width * 5 + units * (2 * (rows + nodes) + 2 * nodes)
    return pl.pallas_call(
        functools.partial(compute_kernel, tile, *scales),
        name="processor",
        out_shape=(
            shape((nodes, width), BF16),
            shape((edges, width), BF16),
            shape((nodes, width), F32),
            shape((edges, width), BF16),
            shape(near.shape, BF16),
            shape(far.shape, BF16),
            shape(w_in.shape, BF16),
            shape(w_out.shape, BF16),
            shape(v_in.shape, BF16),
            shape(v_out.shape, BF16),
        ),
        in_specs=[vmem] * 12,
        out_specs=[vmem] * 10,
        scratch_shapes=[
            pltpu.VMEM((rows + nodes, width), BF16),
            pltpu.VMEM((edges, width), F32),
            pltpu.VMEM((edges, width), F32),
            pltpu.VMEM((edges, 128), F32),
            pltpu.VMEM((edges, width), BF16),
            pltpu.VMEM((nodes, width), F32),
            pltpu.VMEM((nodes, width), BF16),
            pltpu.VMEM((rows + nodes, width), F32),
            pltpu.VMEM((width, width), F32),
            pltpu.VMEM((width, width), F32),
        ],
        compiler_params=pltpu.CompilerParams(vmem_limit_bytes=62 * 1024 * 1024),
        cost_estimate=pl.CostEstimate(flops=work, bytes_accessed=20 * units, transcendentals=units),
    )(
        node,
        edge,
        ncot,
        ecot,
        w_in,
        w_out,
        v_in,
        v_out,
        code.reshape(edges // tile, 1, tile),
        recv.reshape(edges // tile, 1, tile),
        near,
        far,
    )


def bit_count(size):
    bits = size.bit_length() - 1
    assert size == 1 << bits
    return bits


class Swap:
    def __init__(self, sign, near_src, far_src, near_dst, far_dst, sems):
        self.row = lax.axis_index("row")
        self.col = lax.axis_index("col")
        self.rows = lax.axis_size("row")
        self.cols = lax.axis_size("col")
        self.peers = self.rows * self.cols
        self.me = self.row * self.cols + self.col
        self.sign = sign
        self.near = (near_src, near_dst)
        self.far = (far_src, far_dst)
        self.near_send, self.near_recv, self.far_send, self.far_recv, self.own = sems

    def place(self, peer):
        return (peer // self.cols, peer % self.cols)

    def greet(self):
        barrier = pltpu.get_barrier_semaphore()

        def signal(k, carry):
            peer = self.place((self.me + k) % self.peers)
            pl.semaphore_signal(barrier, inc=1, device_id=peer, device_id_type=MESH)
            return carry

        lax.fori_loop(1, self.peers, signal, 0)
        pl.semaphore_wait(barrier, self.peers - 1)

    def near_copy(self, k):
        by = self.sign * (1, -1, 1, -1)[k]
        row, col = self.row, self.col
        if k < 2:
            row = (row + by + self.rows) % self.rows
        else:
            col = (col + by + self.cols) % self.cols
        return pltpu.make_async_remote_copy(
            src_ref=self.near[0].at[k],
            dst_ref=self.near[1].at[k],
            send_sem=self.near_send.at[k],
            recv_sem=self.near_recv.at[k],
            device_id=(row, col),
            device_id_type=MESH,
        )

    def far_copy(self, k):
        peer = (self.me + k) % self.peers
        return pltpu.make_async_remote_copy(
            src_ref=self.far[0].at[peer],
            dst_ref=self.far[1].at[self.me],
            send_sem=self.far_send.at[k],
            recv_sem=self.far_recv.at[k],
            device_id=self.place(peer),
            device_id_type=MESH,
        )

    def own_copy(self):
        return pltpu.make_async_copy(
            self.far[0].at[self.me], self.far[1].at[self.me], self.own.at[0]
        )

    def start(self):
        for k in range(4):
            self.near_copy(k).start()

        def begin(k, carry):
            self.far_copy(k).start()
            return carry

        lax.fori_loop(1, self.peers, begin, 0)
        self.own_copy().start()

    def wait(self):
        for k in range(4):
            self.near_copy(k).wait()

        def end(k, carry):
            self.far_copy(k).wait()
            return carry

        lax.fori_loop(1, self.peers, end, 0)
        self.own_copy().wait()


def swap_sems(peers):
    dma = pltpu.SemaphoreType.DMA
    return [dma((4,)), dma((4,)), dma((peers,)), dma((peers,)), dma((1,))]


def halo_kernel(owner_ref, node_ref, near_ref, far_ref, near_s, far_s, *sems):
    nodes = node_ref.shape[0]
    near_rows = near_s.shape[0] * near_s.shape[1]
    swap = Swap(1, near_s, far_s, near_ref, far_ref, sems)
    offered = cross(col_hot(owner_ref[...], nodes), node_ref[...])
    near_s[...] = offered[:near_rows].reshape(near_s.shape).astype(BF16)
    far_s[...] = offered[near_rows:].reshape(far_s.shape).astype(BF16)
    swap.greet()
    swap.start()
    swap.wait()


def halo(owner, node, near_shape, far_shape):
    vmem = pl.BlockSpec(memory_space=pltpu.VMEM)
    return pl.pallas_call(
        halo_kernel,
        name="halo",
        out_shape=(
            jax.ShapeDtypeStruct(near_shape, BF16),
            jax.ShapeDtypeStruct(far_shape, BF16),
        ),
        in_specs=[vmem] * 2,
        out_specs=[vmem] * 2,
        scratch_shapes=[pltpu.VMEM(near_shape, BF16), pltpu.VMEM(far_shape, BF16)]
        + swap_sems(far_shape[0]),
        compiler_params=pltpu.CompilerParams(collective_id=1, has_side_effects=True),
        cost_estimate=pl.CostEstimate(flops=10**8, bytes_accessed=10**7, transcendentals=0),
    )(owner, node)


def scatter_kernel(orders, row_bits, col_bits, count, *refs):
    bits = row_bits + col_bits
    refs = list(refs)

    def taken(number):
        got = refs[:number]
        del refs[:number]
        return got

    inputs = taken(count)
    near_src, far_src = taken(2)
    outputs = taken(count)
    near_dst, far_dst = taken(2)
    recv = [taken(bits) for _ in range(count)]
    held = [taken(bits) for _ in range(count)]
    send_sem, recv_sem, local_sem = taken(3)
    row = lax.axis_index("row")
    col = lax.axis_index("col")
    swap = Swap(-1, near_src, far_src, near_dst, far_dst, refs)

    def mine(bit):
        if bit < row_bits:
            return (row // (1 << (row_bits - 1 - bit))) % 2
        return (col // (1 << (bits - 1 - bit))) % 2

    def partner(bit):
        if bit < row_bits:
            step = 1 << (row_bits - 1 - bit)
            return (row + step * (1 - 2 * mine(bit)), col)
        step = 1 << (bits - 1 - bit)
        return (row, col + step * (1 - 2 * mine(bit)))

    swap.greet()
    left = [list(range(bits)) for _ in range(count)]
    current = list(inputs)

    def copy_of(a, phase):
        bit = orders[a][phase]
        place = left[a].index(bit)
        spot = (slice(None),) * place + (1 - mine(bit),)
        return pltpu.make_async_remote_copy(
            src_ref=current[a].at[spot],
            dst_ref=recv[a][phase],
            send_sem=send_sem.at[a, phase],
            recv_sem=recv_sem.at[a, phase],
            device_id=partner(bit),
            device_id_type=MESH,
        )

    copies = [copy_of(a, 0) for a in range(count)]
    for item in copies:
        item.start()
    swap.start()
    kept = []
    for a in range(count):
        bit = orders[a][0]
        place = left[a].index(bit)
        spot = (slice(None),) * place + (mine(bit),)
        kept.append(pltpu.make_async_copy(inputs[a].at[spot], held[a][0], local_sem.at[a]))
        kept[a].start()
    sent = []
    for phase in range(bits):
        for a in range(count):
            copies[a].wait_recv()
            sent.append(copies[a])
            bit = orders[a][phase]
            place = left[a].index(bit)
            spot = (slice(None),) * place + (mine(bit),)
            left[a].remove(bit)
            if phase == 0:
                kept[a].wait()
                own = held[a][0][...]
            else:
                own = current[a][spot]
            value = own.astype(F32) + recv[a][phase][...].astype(F32)
            if phase == bits - 1:
                outputs[a][...] = value
            else:
                current[a] = held[a][phase]
                current[a][...] = value.astype(BF16)
                copies[a] = copy_of(a, phase + 1)
                copies[a].start()
    for item in sent:
        item.wait_send()
    swap.wait()


def scatter_sum(grads, near_grad, far_grad):
    rows_grid = lax.axis_size("row")
    cols_grid = lax.axis_size("col")
    row_bits = bit_count(rows_grid)
    col_bits = bit_count(cols_grid)
    bits = row_bits + col_bits
    peers = rows_grid * cols_grid
    width = grads[0].shape[-1]
    slabs = [g.shape[0] // peers for g in grads]
    shaped = [g.reshape((2,) * bits + (s, width)) for g, s in zip(grads, slabs)]
    core = bits - 1
    along_col = list(range(bits - 2, row_bits - 1, -1))
    row_near = [row_bits - 1]
    row_far = list(range(row_bits - 2, -1, -1))
    turns = [
        [core] + along_col + row_near + row_far,
        [core] + row_near + row_far + along_col,
        [core] + row_far + along_col + row_near,
        [core] + row_far + along_col + row_near,
    ]
    count = len(grads)
    vmem = pl.BlockSpec(memory_space=pltpu.VMEM)
    anywhere = pl.BlockSpec(memory_space=pl.ANY)
    recv = [
        pltpu.VMEM((2,) * (bits - 1 - phase) + (s, width), BF16)
        for s in slabs
        for phase in range(bits)
    ]
    shape = jax.ShapeDtypeStruct
    dma = pltpu.SemaphoreType.DMA
    return pl.pallas_call(
        functools.partial(scatter_kernel, turns, row_bits, col_bits, count),
        name="scatter_sum",
        out_shape=tuple(shape((s, width), F32) for s in slabs)
        + (shape(near_grad.shape, BF16), shape(far_grad.shape, BF16)),
        in_specs=[anywhere] * count + [vmem] * 2,
        out_specs=[vmem] * (count + 2),
        scratch_shapes=recv
        + recv
        + [dma((count, bits)), dma((count, bits)), dma((count,))]
        + swap_sems(peers),
        compiler_params=pltpu.CompilerParams(
            collective_id=0, has_side_effects=True, vmem_limit_bytes=40 * 1024 * 1024
        ),
        cost_estimate=pl.CostEstimate(flops=10**9, bytes_accessed=10**8, transcendentals=0),
    )(*shaped, near_grad, far_grad)


def finish_kernel(count, owner_ref, part_ref, near_ref, far_ref, *refs):
    nodes = part_ref.shape[0]
    near = near_ref.shape[0]
    sums = refs[:count]
    grad_ref = refs[count]
    hot = col_hot(owner_ref[...], nodes)
    total = part_ref[...] + dot(hot[:, :near], near_ref[...])
    grad_ref[...] = (total + dot(hot[:, near:], far_ref[...])).astype(BF16)
    for source, target in zip(sums, refs[count + 1 :]):
        target[...] = source[...]


def finish(owner, part, near, far, sums):
    vmem = pl.BlockSpec(memory_space=pltpu.VMEM)
    count = len(sums)
    return pl.pallas_call(
        functools.partial(finish_kernel, count),
        name="finish",
        out_shape=(jax.ShapeDtypeStruct(part.shape, BF16),)
        + tuple(jax.ShapeDtypeStruct(item.shape, F32) for item in sums),
        in_specs=[vmem] * (4 + count),
        out_specs=[vmem] * (1 + count),
    )(owner, part, near, far, *sums)


def shards(
    node_latent,
    edge_latent,
    node_cotangent,
    edge_cotangent,
    w_edge_in,
    w_edge_out,
    w_node_in,
    w_node_out,
    sender_code,
    receiver,
    near_list,
    far_list,
):
    node_rows, width = node_latent.shape
    edge_rows = edge_latent.shape[0]
    peers = lax.axis_size("row") * lax.axis_size("col")
    near_shape = (4, near_list.shape[2], width)
    far_shape = (peers, far_list.shape[2], width)
    owner = jnp.concatenate([near_list.reshape(-1), far_list.reshape(-1)], 0)[None, :]
    near, far = halo(owner, node_latent, near_shape, far_shape)
    scales = (1.0 / math.sqrt(edge_rows * peers), 1.0 / math.sqrt(node_rows * peers))
    node_new, edge_new, part, grad_edge, near_grad, far_grad, g_in, g_out, h_in, h_out = compute(
        node_latent,
        edge_latent,
        node_cotangent,
        edge_cotangent,
        w_edge_in,
        w_edge_out,
        w_node_in,
        w_node_out,
        sender_code,
        receiver,
        near.reshape(-1, width),
        far.reshape(-1, width),
        scales,
    )
    *sums, near_back, far_back = scatter_sum(
        (g_in, h_in, g_out, h_out), near_grad.reshape(near_shape), far_grad.reshape(far_shape)
    )
    grad_node, s_in, s_hin, s_out, s_hout = finish(
        owner, part, near_back.reshape(-1, width), far_back.reshape(-1, width), sums
    )
    return (node_new, edge_new, grad_node, grad_edge, s_in, s_out, s_hin, s_hout)


def solution(mesh):
    both = ("row", "col")
    in_specs = (
        P(both, None),
        P(both, None),
        P(both, None),
        P(both, None),
        P(),
        P(),
        P(),
        P(),
        P(both),
        P(both),
        P(both, None, None),
        P(both, None, None),
    )
    out_specs = (P(both, None),) * 8
    return jax.shard_map(shards, mesh=mesh, in_specs=in_specs, out_specs=out_specs, check_vma=False)
```

```python
import functools
import math

import jax
import jax.numpy as jnp
from jax import lax
from jax.experimental import pallas as pl
from jax.experimental.pallas import tpu as pltpu
from jax.sharding import PartitionSpec as P

EPS = 1e-05
MESH = pl.DeviceIdType.MESH
F32 = jnp.float32
BF16 = jnp.bfloat16


def dot(left, right):
    return jnp.dot(left, right, preferred_element_type=F32)


def dot_t(left, weight):
    return lax.dot_general(left, weight, (((1,), (1,)), ((), ())), preferred_element_type=F32)


def cross(left, right):
    return lax.dot_general(left, right, (((0,), (0,)), ((), ())), preferred_element_type=F32)


def norm_parts(value):
    mean = jnp.mean(value, -1, keepdims=True)
    centred = value - mean
    recip = lax.rsqrt(jnp.mean(centred * centred, -1, keepdims=True) + EPS)
    return centred * recip, recip


def norm_back(normed, recip, grad):
    inner = (
        grad
        - jnp.mean(grad, -1, keepdims=True)
        - normed * jnp.mean(grad * normed, -1, keepdims=True)
    )
    return recip * inner


def row_hot(codes, count):
    tile = codes.shape[1]
    column = jnp.transpose(jnp.broadcast_to(codes, (128, tile)))
    lane = lax.broadcasted_iota(jnp.int32, (tile, 128), 1)
    groups = [
        jnp.where(column == lane + 128 * g, 1.0, 0.0).astype(BF16) for g in range(count // 128)
    ]
    return jnp.concatenate(groups, 1)


def col_hot(codes, count):
    tile = codes.shape[1]
    ids = lax.broadcasted_iota(jnp.int32, (count, tile), 0)
    return jnp.where(codes == ids, 1.0, 0.0).astype(BF16)


def compute_kernel(
    tile,
    edge_scale,
    node_scale,
    node_ref,
    edge_ref,
    ncot_ref,
    ecot_ref,
    w_in,
    w_out,
    v_in,
    v_out,
    code_ref,
    recv_ref,
    near_ref,
    far_ref,
    node_new_ref,
    edge_new_ref,
    part_ref,
    grad_edge_ref,
    near_grad_ref,
    far_grad_ref,
    g_in_ref,
    g_out_ref,
    h_in_ref,
    h_out_ref,
    proj,
    slope,
    normed_s,
    recip_s,
    hidden_s,
    gath_s,
    gg_s,
    sums_s,
    acc_e,
    acc_o,
):
    nodes, width = node_ref.shape
    edges = edge_ref.shape[0]
    near = near_ref.shape[0]
    far = far_ref.shape[0]
    rows = nodes + near + far
    steps = edges // tile
    w_e = w_in.at[pl.ds(0, width)]
    w_s = w_in.at[pl.ds(width, width)]
    w_r = w_in.at[pl.ds(2 * width, width)]
    v_a = v_in.at[pl.ds(0, width)]
    v_b = v_in.at[pl.ds(width, width)]
    proj[pl.ds(0, nodes), :] = dot(node_ref[...], w_s[...]).astype(BF16)
    proj[pl.ds(nodes, near), :] = dot(near_ref[...], w_s[...]).astype(BF16)
    proj[pl.ds(nodes + near, far), :] = dot(far_ref[...], w_s[...]).astype(BF16)
    proj[pl.ds(rows, nodes), :] = dot(node_ref[...], w_r[...]).astype(BF16)
    gath_s[...] = jnp.zeros_like(gath_s)

    def forward(step, carry):
        span = pl.ds(pl.multiple_of(step * tile, tile), tile)
        codes = code_ref[step]
        recvs = recv_ref[step]
        hot = jnp.concatenate([row_hot(codes, rows), row_hot(recvs, nodes)], 1)
        edge = edge_ref[span, :]
        pre = dot(edge, w_e[...]) + dot(hot, proj[...])
        sigma = jax.nn.sigmoid(pre)
        slope[span, :] = sigma * (1.0 + pre * (1.0 - sigma))
        hidden = (pre * sigma).astype(BF16)
        hidden_s[span, :] = hidden
        normed, recip = norm_parts(dot(hidden, w_out[...]))
        normed_s[span, :] = normed
        recip_s[span, :] = jnp.broadcast_to(recip, (tile, 128))
        new = (edge.astype(F32) + normed).astype(BF16)
        edge_new_ref[span, :] = new
        gath_s[...] += dot(col_hot(recvs, nodes), new)
        return carry

    lax.fori_loop(0, steps, forward, 0)

    node = node_ref[...]
    gathered = gath_s[...].astype(BF16)
    pre = dot(node, v_a[...]) + dot(gathered, v_b[...])
    sigma = jax.nn.sigmoid(pre)
    hidden = (pre * sigma).astype(BF16)
    normed, recip = norm_parts(dot(hidden, v_out[...]))
    node_new_ref[...] = (node.astype(F32) + normed).astype(BF16)
    ncot = ncot_ref[...].astype(F32)
    delta = norm_back(normed, recip, ncot).astype(BF16)
    pre_delta = (dot_t(delta, v_out[...]) * (sigma * (1.0 + pre * (1.0 - sigma)))).astype(BF16)
    gg_s[...] = dot_t(pre_delta, v_b[...]).astype(BF16)
    part_ref[...] = ncot + dot_t(pre_delta, v_a[...])
    h_in_ref[pl.ds(0, width), :] = (cross(node, pre_delta) * node_scale).astype(BF16)
    h_in_ref[pl.ds(width, width), :] = (cross(gathered, pre_delta) * node_scale).astype(BF16)
    h_out_ref[...] = (cross(hidden, delta) * node_scale).astype(BF16)

    sums_s[...] = jnp.zeros_like(sums_s)
    acc_e[...] = jnp.zeros_like(acc_e)
    acc_o[...] = jnp.zeros_like(acc_o)

    def backward(step, carry):
        span = pl.ds(pl.multiple_of(step * tile, tile), tile)
        codes = code_ref[step]
        recvs = recv_ref[step]
        total = ecot_ref[span, :].astype(F32) + dot(row_hot(recvs, nodes), gg_s[...])
        recip = recip_s[span, :][:, :1]
        delta = norm_back(normed_s[span, :], recip, total).astype(BF16)
        pre_delta = (dot_t(delta, w_out[...]) * slope[span, :]).astype(BF16)
        grad_edge_ref[span, :] = (total + dot_t(pre_delta, w_e[...])).astype(BF16)
        hot = jnp.concatenate([col_hot(codes, rows), col_hot(recvs, nodes)], 0)
        sums_s[...] += dot(hot, pre_delta)
        acc_e[...] += cross(edge_ref[span, :], pre_delta)
        acc_o[...] += cross(hidden_s[span, :], delta)
        return carry

    lax.fori_loop(0, steps, backward, 0)

    g_in_ref[pl.ds(0, width), :] = (acc_e[...] * edge_scale).astype(BF16)
    g_out_ref[...] = (acc_o[...] * edge_scale).astype(BF16)
    own_sum = sums_s[pl.ds(0, nodes), :].astype(BF16)
    near_sum = sums_s[pl.ds(nodes, near), :].astype(BF16)
    far_sum = sums_s[pl.ds(nodes + near, far), :].astype(BF16)
    recv_sum = sums_s[pl.ds(rows, nodes), :].astype(BF16)
    near_grad_ref[...] = dot_t(near_sum, w_s[...]).astype(BF16)
    far_grad_ref[...] = dot_t(far_sum, w_s[...]).astype(BF16)
    part_ref[...] += dot_t(own_sum, w_s[...]) + dot_t(recv_sum, w_r[...])
    sent = cross(node_ref[...], own_sum) + cross(near_ref[...], near_sum)
    sent += cross(far_ref[...], far_sum)
    g_in_ref[pl.ds(width, width), :] = (sent * edge_scale).astype(BF16)
    g_in_ref[pl.ds(2 * width, width), :] = (cross(node_ref[...], recv_sum) * edge_scale).astype(BF16)


def compute(node, edge, ncot, ecot, w_in, w_out, v_in, v_out, code, recv, near, far, scales):
    nodes, width = node.shape
    edges = edge.shape[0]
    rows = nodes + near.shape[0] + far.shape[0]
    tile = math.gcd(edges, 512)
    vmem = pl.BlockSpec(memory_space=pltpu.VMEM)
    shape = jax.ShapeDtypeStruct
    units = 2 * edges * width
    work = units * width * 5 + units * (2 * (rows + nodes) + 2 * nodes)
    return pl.pallas_call(
        functools.partial(compute_kernel, tile, *scales),
        name="processor",
        out_shape=(
            shape((nodes, width), BF16),
            shape((edges, width), BF16),
            shape((nodes, width), F32),
            shape((edges, width), BF16),
            shape(near.shape, BF16),
            shape(far.shape, BF16),
            shape(w_in.shape, BF16),
            shape(w_out.shape, BF16),
            shape(v_in.shape, BF16),
            shape(v_out.shape, BF16),
        ),
        in_specs=[vmem] * 12,
        out_specs=[vmem] * 10,
        scratch_shapes=[
            pltpu.VMEM((rows + nodes, width), BF16),
            pltpu.VMEM((edges, width), F32),
            pltpu.VMEM((edges, width), F32),
            pltpu.VMEM((edges, 128), F32),
            pltpu.VMEM((edges, width), BF16),
            pltpu.VMEM((nodes, width), F32),
            pltpu.VMEM((nodes, width), BF16),
            pltpu.VMEM((rows + nodes, width), F32),
            pltpu.VMEM((width, width), F32),
            pltpu.VMEM((width, width), F32),
        ],
        compiler_params=pltpu.CompilerParams(vmem_limit_bytes=62 * 1024 * 1024),
        cost_estimate=pl.CostEstimate(flops=work, bytes_accessed=20 * units, transcendentals=units),
    )(
        node,
        edge,
        ncot,
        ecot,
        w_in,
        w_out,
        v_in,
        v_out,
        code.reshape(edges // tile, 1, tile),
        recv.reshape(edges // tile, 1, tile),
        near,
        far,
    )


def bit_count(size):
    bits = size.bit_length() - 1
    assert size == 1 << bits
    return bits


class Swap:
    def __init__(self, sign, near_src, far_src, near_dst, far_dst, sems):
        self.row = lax.axis_index("row")
        self.col = lax.axis_index("col")
        self.rows = lax.axis_size("row")
        self.cols = lax.axis_size("col")
        self.peers = self.rows * self.cols
        self.me = self.row * self.cols + self.col
        self.sign = sign
        self.near = (near_src, near_dst)
        self.far = (far_src, far_dst)
        self.near_send, self.near_recv, self.far_send, self.far_recv, self.own = sems

    def place(self, peer):
        return (peer // self.cols, peer % self.cols)

    def greet(self):
        barrier = pltpu.get_barrier_semaphore()

        def signal(k, carry):
            peer = self.place((self.me + k) % self.peers)
            pl.semaphore_signal(barrier, inc=1, device_id=peer, device_id_type=MESH)
            return carry

        lax.fori_loop(1, self.peers, signal, 0)
        pl.semaphore_wait(barrier, self.peers - 1)

    def near_copy(self, k):
        by = self.sign * (1, -1, 1, -1)[k]
        row, col = self.row, self.col
        if k < 2:
            row = (row + by + self.rows) % self.rows
        else:
            col = (col + by + self.cols) % self.cols
        return pltpu.make_async_remote_copy(
            src_ref=self.near[0].at[k],
            dst_ref=self.near[1].at[k],
            send_sem=self.near_send.at[k],
            recv_sem=self.near_recv.at[k],
            device_id=(row, col),
            device_id_type=MESH,
        )

    def far_copy(self, k):
        peer = (self.me + k) % self.peers
        return pltpu.make_async_remote_copy(
            src_ref=self.far[0].at[peer],
            dst_ref=self.far[1].at[self.me],
            send_sem=self.far_send.at[k],
            recv_sem=self.far_recv.at[k],
            device_id=self.place(peer),
            device_id_type=MESH,
        )

    def own_copy(self):
        return pltpu.make_async_copy(
            self.far[0].at[self.me], self.far[1].at[self.me], self.own.at[0]
        )

    def start(self):
        for k in range(4):
            self.near_copy(k).start()

        def begin(k, carry):
            self.far_copy(k).start()
            return carry

        lax.fori_loop(1, self.peers, begin, 0)
        self.own_copy().start()

    def wait(self):
        for k in range(4):
            self.near_copy(k).wait()

        def end(k, carry):
            self.far_copy(k).wait()
            return carry

        lax.fori_loop(1, self.peers, end, 0)
        self.own_copy().wait()


def swap_sems(peers):
    dma = pltpu.SemaphoreType.DMA
    return [dma((4,)), dma((4,)), dma((peers,)), dma((peers,)), dma((1,))]


def halo_kernel(owner_ref, node_ref, near_ref, far_ref, near_s, far_s, *sems):
    nodes = node_ref.shape[0]
    near_rows = near_s.shape[0] * near_s.shape[1]
    swap = Swap(1, near_s, far_s, near_ref, far_ref, sems)
    offered = cross(col_hot(owner_ref[...], nodes), node_ref[...])
    near_s[...] = offered[:near_rows].reshape(near_s.shape).astype(BF16)
    far_s[...] = offered[near_rows:].reshape(far_s.shape).astype(BF16)
    swap.greet()
    swap.start()
    swap.wait()


def halo(owner, node, near_shape, far_shape):
    vmem = pl.BlockSpec(memory_space=pltpu.VMEM)
    return pl.pallas_call(
        halo_kernel,
        name="halo",
        out_shape=(
            jax.ShapeDtypeStruct(near_shape, BF16),
            jax.ShapeDtypeStruct(far_shape, BF16),
        ),
        in_specs=[vmem] * 2,
        out_specs=[vmem] * 2,
        scratch_shapes=[pltpu.VMEM(near_shape, BF16), pltpu.VMEM(far_shape, BF16)]
        + swap_sems(far_shape[0]),
        compiler_params=pltpu.CompilerParams(collective_id=1, has_side_effects=True),
        cost_estimate=pl.CostEstimate(flops=10**8, bytes_accessed=10**7, transcendentals=0),
    )(owner, node)


def scatter_kernel(orders, row_bits, col_bits, count, *refs):
    bits = row_bits + col_bits
    refs = list(refs)

    def taken(number):
        got = refs[:number]
        del refs[:number]
        return got

    inputs = taken(count)
    near_src, far_src = taken(2)
    outputs = taken(count)
    near_dst, far_dst = taken(2)
    recv = [taken(bits) for _ in range(count)]
    held = [taken(bits) for _ in range(count)]
    send_sem, recv_sem, local_sem = taken(3)
    row = lax.axis_index("row")
    col = lax.axis_index("col")
    swap = Swap(-1, near_src, far_src, near_dst, far_dst, refs)

    def mine(bit):
        if bit < row_bits:
            return (row // (1 << (row_bits - 1 - bit))) % 2
        return (col // (1 << (bits - 1 - bit))) % 2

    def partner(bit):
        if bit < row_bits:
            step = 1 << (row_bits - 1 - bit)
            return (row + step * (1 - 2 * mine(bit)), col)
        step = 1 << (bits - 1 - bit)
        return (row, col + step * (1 - 2 * mine(bit)))

    swap.greet()
    left = [list(range(bits)) for _ in range(count)]
    current = list(inputs)

    def copy_of(a, phase):
        bit = orders[a][phase]
        place = left[a].index(bit)
        spot = (slice(None),) * place + (1 - mine(bit),)
        return pltpu.make_async_remote_copy(
            src_ref=current[a].at[spot],
            dst_ref=recv[a][phase],
            send_sem=send_sem.at[a, phase],
            recv_sem=recv_sem.at[a, phase],
            device_id=partner(bit),
            device_id_type=MESH,
        )

    copies = [copy_of(a, 0) for a in range(count)]
    for item in copies:
        item.start()
    swap.start()
    kept = []
    for a in range(count):
        bit = orders[a][0]
        place = left[a].index(bit)
        spot = (slice(None),) * place + (mine(bit),)
        kept.append(pltpu.make_async_copy(inputs[a].at[spot], held[a][0], local_sem.at[a]))
        kept[a].start()
    sent = []
    for phase in range(bits):
        for a in range(count):
            copies[a].wait_recv()
            sent.append(copies[a])
            bit = orders[a][phase]
            place = left[a].index(bit)
            spot = (slice(None),) * place + (mine(bit),)
            left[a].remove(bit)
            if phase == 0:
                kept[a].wait()
                own = held[a][0][...]
            else:
                own = current[a][spot]
            value = own.astype(F32) + recv[a][phase][...].astype(F32)
            if phase == bits - 1:
                outputs[a][...] = value
            else:
                current[a] = held[a][phase]
                current[a][...] = value.astype(BF16)
                copies[a] = copy_of(a, phase + 1)
                copies[a].start()
    for item in sent:
        item.wait_send()
    swap.wait()


def scatter_sum(grads, near_grad, far_grad):
    rows_grid = lax.axis_size("row")
    cols_grid = lax.axis_size("col")
    row_bits = bit_count(rows_grid)
    col_bits = bit_count(cols_grid)
    bits = row_bits + col_bits
    peers = rows_grid * cols_grid
    width = grads[0].shape[-1]
    slabs = [g.shape[0] // peers for g in grads]
    shaped = [g.reshape((2,) * bits + (s, width)) for g, s in zip(grads, slabs)]
    core = bits - 1
    along_col = list(range(bits - 2, row_bits - 1, -1))
    row_near = [row_bits - 1]
    row_far = list(range(row_bits - 2, -1, -1))
    turns = [
        [core] + along_col + row_near + row_far,
        [core] + row_near + row_far + along_col,
        [core] + row_far + along_col + row_near,
        [core] + row_far + along_col + row_near,
    ]
    count = len(grads)
    vmem = pl.BlockSpec(memory_space=pltpu.VMEM)
    anywhere = pl.BlockSpec(memory_space=pl.ANY)
    recv = [
        pltpu.VMEM((2,) * (bits - 1 - phase) + (s, width), BF16)
        for s in slabs
        for phase in range(bits)
    ]
    shape = jax.ShapeDtypeStruct
    dma = pltpu.SemaphoreType.DMA
    return pl.pallas_call(
        functools.partial(scatter_kernel, turns, row_bits, col_bits, count),
        name="scatter_sum",
        out_shape=tuple(shape((s, width), F32) for s in slabs)
        + (shape(near_grad.shape, BF16), shape(far_grad.shape, BF16)),
        in_specs=[anywhere] * count + [vmem] * 2,
        out_specs=[vmem] * (count + 2),
        scratch_shapes=recv
        + recv
        + [dma((count, bits)), dma((count, bits)), dma((count,))]
        + swap_sems(peers),
        compiler_params=pltpu.CompilerParams(
            collective_id=0, has_side_effects=True, vmem_limit_bytes=40 * 1024 * 1024
        ),
        cost_estimate=pl.CostEstimate(flops=10**9, bytes_accessed=10**8, transcendentals=0),
    )(*shaped, near_grad, far_grad)


def finish_kernel(count, owner_ref, part_ref, near_ref, far_ref, *refs):
    nodes = part_ref.shape[0]
    near = near_ref.shape[0]
    sums = refs[:count]
    grad_ref = refs[count]
    hot = col_hot(owner_ref[...], nodes)
    total = part_ref[...] + dot(hot[:, :near], near_ref[...])
    grad_ref[...] = (total + dot(hot[:, near:], far_ref[...])).astype(BF16)
    for source, target in zip(sums, refs[count + 1 :]):
        target[...] = source[...]


def finish(owner, part, near, far, sums):
    vmem = pl.BlockSpec(memory_space=pltpu.VMEM)
    count = len(sums)
    return pl.pallas_call(
        functools.partial(finish_kernel, count),
        name="finish",
        out_shape=(jax.ShapeDtypeStruct(part.shape, BF16),)
        + tuple(jax.ShapeDtypeStruct(item.shape, F32) for item in sums),
        in_specs=[vmem] * (4 + count),
        out_specs=[vmem] * (1 + count),
    )(owner, part, near, far, *sums)


class Halving:
    def __init__(self, order, row_bits, col_bits, source, recv, held, out, send_sem, recv_sem):
        self.order = order
        self.row_bits = row_bits
        self.bits = row_bits + col_bits
        self.left = list(range(self.bits))
        self.current = source
        self.recv, self.held, self.out = recv, held, out
        self.send_sem, self.recv_sem = send_sem, recv_sem
        self.sent = []
        self.phase = 0

    def mine(self, bit):
        if bit < self.row_bits:
            return (lax.axis_index("row") // (1 << (self.row_bits - 1 - bit))) % 2
        return (lax.axis_index("col") // (1 << (self.bits - 1 - bit))) % 2

    def partner(self, bit):
        row, col = lax.axis_index("row"), lax.axis_index("col")
        if bit < self.row_bits:
            return (row + (1 << (self.row_bits - 1 - bit)) * (1 - 2 * self.mine(bit)), col)
        return (row, col + (1 << (self.bits - 1 - bit)) * (1 - 2 * self.mine(bit)))

    def spot(self, bit, which):
        return (slice(None),) * self.left.index(bit) + (which,)

    def start(self):
        bit = self.order[self.phase]
        copy = pltpu.make_async_remote_copy(
            src_ref=self.current.at[self.spot(bit, 1 - self.mine(bit))],
            dst_ref=self.recv[self.phase],
            send_sem=self.send_sem.at[self.phase],
            recv_sem=self.recv_sem.at[self.phase],
            device_id=self.partner(bit),
            device_id_type=MESH,
        )
        copy.start()
        self.sent.append(copy)

    def step(self):
        bit = self.order[self.phase]
        self.sent[-1].wait_recv()
        own = self.current[self.spot(bit, self.mine(bit))]
        value = own.astype(F32) + self.recv[self.phase][...].astype(F32)
        self.left.remove(bit)
        self.phase += 1
        if self.phase == self.bits:
            self.out[...] = value
            return
        self.current = self.held[self.phase - 1]
        self.current[...] = value.astype(BF16)
        self.start()

    def end(self):
        for copy in self.sent:
            copy.wait_send()


def whole_kernel(tile, scales, turns, row_bits, col_bits, *refs):
    edge_scale, node_scale = scales
    bits = row_bits + col_bits
    refs = list(refs)

    def taken(number):
        got = refs[:number]
        del refs[:number]
        return got

    owner_ref, node_ref, ncot_ref, code_ref, recv_ref = taken(5)
    loads = taken(6)
    node_new_ref, edge_new_ref, grad_edge_ref, part_ref, near_back, far_back = taken(6)
    outputs = taken(4)
    proj, slope, normed_s, recip_s, hidden_s, gath_s, gg_s, sums_s, acc_e, acc_o = taken(10)
    held_in = taken(6)
    edge_new_s, grad_edge_s = taken(2)
    near_s, far_s, near_r, far_r, near_g, far_g = taken(6)
    grads = taken(4)
    recv = [taken(bits) for _ in range(4)]
    held = [taken(bits - 1) for _ in range(4)]
    send_sem, recv_sem, load_sem, store_sem = taken(4)
    out_swap = Swap(1, near_s, far_s, near_r, far_r, taken(5))
    back_swap = Swap(-1, near_g, far_g, near_back, far_back, taken(5))

    copies = []
    for k in (0, 2, 3, 4, 5, 1):
        copies.append(pltpu.make_async_copy(loads[k], held_in[k], load_sem.at[k]))
        copies[-1].start()
    edge_s, ecot_s, w_in, w_out, v_in, v_out = held_in
    edge_copy, w_in_copy, w_out_copy, v_in_copy, v_out_copy, ecot_copy = copies

    nodes, width = node_ref.shape
    edges = edge_s.shape[0]
    near = near_s.shape[0] * near_s.shape[1]
    far = far_s.shape[0] * far_s.shape[1]
    rows = nodes + near + far
    steps = edges // tile
    w_e = w_in.at[pl.ds(0, width)]
    w_s = w_in.at[pl.ds(width, width)]
    w_r = w_in.at[pl.ds(2 * width, width)]
    v_a = v_in.at[pl.ds(0, width)]
    v_b = v_in.at[pl.ds(width, width)]

    def span_of(step):
        return pl.ds(pl.multiple_of(step * tile, tile), tile)

    offered = cross(col_hot(owner_ref[...], nodes), node_ref[...])
    near_s[...] = offered[:near].reshape(near_s.shape).astype(BF16)
    far_s[...] = offered[near:].reshape(far_s.shape).astype(BF16)
    out_swap.greet()
    out_swap.start()

    edge_copy.wait()
    w_in_copy.wait()
    gath_s[...] = jnp.zeros_like(gath_s)
    sums_s[...] = jnp.zeros_like(sums_s)
    acc_e[...] = jnp.zeros_like(acc_e)
    acc_o[...] = jnp.zeros_like(acc_o)
    proj[pl.ds(0, nodes), :] = dot(node_ref[...], w_s[...]).astype(BF16)
    proj[pl.ds(rows, nodes), :] = dot(node_ref[...], w_r[...]).astype(BF16)

    def ahead(step, carry):
        span = span_of(step)
        hot = row_hot(recv_ref[step], nodes)
        slope[span, :] = dot(edge_s[span, :], w_e[...]) + dot(hot, proj[pl.ds(rows, nodes), :])
        return carry

    lax.fori_loop(0, steps, ahead, 0)
    w_out_copy.wait()
    v_in_copy.wait()
    v_out_copy.wait()
    ecot_copy.wait()
    out_swap.wait()
    near_rows = near_r[...].astype(F32).reshape(near, width).astype(BF16)
    far_rows = far_r[...].astype(F32).reshape(far, width).astype(BF16)
    proj[pl.ds(nodes, near), :] = dot(near_rows, w_s[...]).astype(BF16)
    proj[pl.ds(nodes + near, far), :] = dot(far_rows, w_s[...]).astype(BF16)

    def forward(step, carry):
        span = span_of(step)
        edge = edge_s[span, :]
        pre = slope[span, :] + dot(row_hot(code_ref[step], rows), proj[pl.ds(0, rows), :])
        sigma = jax.nn.sigmoid(pre)
        slope[span, :] = sigma * (1.0 + pre * (1.0 - sigma))
        hidden = (pre * sigma).astype(BF16)
        hidden_s[span, :] = hidden
        normed, recip = norm_parts(dot(hidden, w_out[...]))
        normed_s[span, :] = normed
        recip_s[span, :] = jnp.broadcast_to(recip, (tile, 128))
        new = (edge.astype(F32) + normed).astype(BF16)
        edge_new_s[span, :] = new
        gath_s[...] += dot(col_hot(recv_ref[step], nodes), new)
        return carry

    lax.fori_loop(0, steps, forward, 0)
    edge_new_copy = pltpu.make_async_copy(edge_new_s, edge_new_ref, store_sem.at[0])
    edge_new_copy.start()

    node = node_ref[...]
    gathered = gath_s[...].astype(BF16)
    pre = dot(node, v_a[...]) + dot(gathered, v_b[...])
    sigma = jax.nn.sigmoid(pre)
    hidden = (pre * sigma).astype(BF16)
    normed, recip = norm_parts(dot(hidden, v_out[...]))
    node_new_ref[...] = (node.astype(F32) + normed).astype(BF16)
    ncot = ncot_ref[...].astype(F32)
    delta = norm_back(normed, recip, ncot).astype(BF16)
    pre_delta = (dot_t(delta, v_out[...]) * (sigma * (1.0 + pre * (1.0 - sigma)))).astype(BF16)
    g_in, h_in, g_out, h_out = grads
    h_in[pl.ds(0, width), :] = (cross(node, pre_delta) * node_scale).astype(BF16)
    h_in[pl.ds(width, width), :] = (cross(gathered, pre_delta) * node_scale).astype(BF16)
    h_out[...] = (cross(hidden, delta) * node_scale).astype(BF16)

    halvings = []
    for a in range(4):
        slab, _ = outputs[a].shape
        source = grads[a].reshape((2,) * bits + (slab, width))
        halvings.append(
            Halving(
                turns[a],
                row_bits,
                col_bits,
                source,
                recv[a],
                held[a],
                outputs[a],
                send_sem.at[a],
                recv_sem.at[a],
            )
        )
    from_edges = (halvings[0], halvings[2])
    from_nodes = (halvings[1], halvings[3])
    for item in from_nodes:
        item.start()
    gg_s[...] = dot_t(pre_delta, v_b[...]).astype(BF16)
    part_ref[...] = ncot + dot_t(pre_delta, v_a[...])

    def backward(step, carry):
        span = span_of(step)
        recvs = recv_ref[step]
        total = ecot_s[span, :].astype(F32) + dot(row_hot(recvs, nodes), gg_s[...])
        recip = recip_s[span, :][:, :1]
        delta = norm_back(normed_s[span, :], recip, total).astype(BF16)
        normed_s[span, :] = total
        pre_delta = (dot_t(delta, w_out[...]) * slope[span, :]).astype(BF16)
        acc_o[...] += cross(hidden_s[span, :], delta)
        hidden_s[span, :] = pre_delta
        sums_s[pl.ds(0, rows), :] += dot(col_hot(code_ref[step], rows), pre_delta)
        sums_s[pl.ds(rows, nodes), :] += dot(col_hot(recvs, nodes), pre_delta)
        acc_e[...] += cross(edge_s[span, :], pre_delta)
        return carry

    half = steps // 2
    lax.fori_loop(0, half, backward, 0)
    for item in from_nodes:
        item.step()
    lax.fori_loop(half, steps, backward, 0)
    for item in from_nodes:
        item.step()

    g_in[pl.ds(0, width), :] = (acc_e[...] * edge_scale).astype(BF16)
    g_out[...] = (acc_o[...] * edge_scale).astype(BF16)
    own_sum = sums_s[pl.ds(0, nodes), :].astype(BF16)
    near_sum = sums_s[pl.ds(nodes, near), :].astype(BF16)
    far_sum = sums_s[pl.ds(nodes + near, far), :].astype(BF16)
    recv_sum = sums_s[pl.ds(rows, nodes), :].astype(BF16)
    sent = cross(node, own_sum) + cross(near_rows, near_sum) + cross(far_rows, far_sum)
    g_in[pl.ds(width, width), :] = (sent * edge_scale).astype(BF16)
    g_in[pl.ds(2 * width, width), :] = (cross(node, recv_sum) * edge_scale).astype(BF16)
    for item in from_edges:
        item.start()
    near_g[...] = dot_t(near_sum, w_s[...]).reshape(near_g.shape).astype(BF16)
    far_g[...] = dot_t(far_sum, w_s[...]).reshape(far_g.shape).astype(BF16)
    back_swap.start()
    part_ref[...] += dot_t(own_sum, w_s[...]) + dot_t(recv_sum, w_r[...])

    def behind(step, carry):
        span = span_of(step)
        change = dot_t(hidden_s[span, :], w_e[...])
        grad_edge_s[span, :] = (normed_s[span, :] + change).astype(BF16)
        return carry

    lax.fori_loop(0, steps, behind, 0)
    grad_edge_copy = pltpu.make_async_copy(grad_edge_s, grad_edge_ref, store_sem.at[1])
    grad_edge_copy.start()
    for phase in range(bits):
        for item in halvings:
            if item.phase <= phase:
                item.step()
    for item in halvings:
        item.end()
    back_swap.wait()
    edge_new_copy.wait()
    grad_edge_copy.wait()


def whole(owner, node, ncot, code, recv_at, big, near_shape, far_shape, scales):
    row_bits = bit_count(lax.axis_size("row"))
    col_bits = bit_count(lax.axis_size("col"))
    bits = row_bits + col_bits
    peers = 1 << bits
    nodes, width = node.shape
    edges = big[0].shape[0]
    rows = nodes + near_shape[0] * near_shape[1] + far_shape[0] * far_shape[1]
    tile = math.gcd(edges, 512)
    grad_shapes = [big[2].shape, big[4].shape, big[3].shape, big[5].shape]
    slabs = [item[0] // peers for item in grad_shapes]
    core = bits - 1
    along_col = list(range(bits - 2, row_bits - 1, -1))
    row_near = [row_bits - 1]
    row_far = list(range(row_bits - 2, -1, -1))
    turns = [
        [core] + along_col + row_near + row_far,
        [core] + row_near + row_far + along_col,
        [core] + row_near + row_far + along_col,
        [core] + row_far + along_col + row_near,
    ]
    vmem = pl.BlockSpec(memory_space=pltpu.VMEM)
    anywhere = pl.BlockSpec(memory_space=pl.ANY)
    shape = jax.ShapeDtypeStruct
    dma = pltpu.SemaphoreType.DMA
    scratch = pltpu.VMEM
    return pl.pallas_call(
        functools.partial(whole_kernel, tile, scales, turns, row_bits, col_bits),
        name="whole_step",
        out_shape=(
            shape((nodes, width), BF16),
            shape((edges, width), BF16),
            shape((edges, width), BF16),
            shape((nodes, width), F32),
            shape(near_shape, BF16),
            shape(far_shape, BF16),
        )
        + tuple(shape((s, width), F32) for s in slabs),
        in_specs=[vmem] * 5 + [anywhere] * 6,
        out_specs=[vmem, anywhere, anywhere] + [vmem] * 7,
        scratch_shapes=[
            scratch((rows + nodes, width), BF16),
            scratch((edges, width), F32),
            scratch((edges, width), F32),
            scratch((edges, 128), F32),
            scratch((edges, width), BF16),
            scratch((nodes, width), F32),
            scratch((nodes, width), BF16),
            scratch((rows + nodes, width), F32),
            scratch((width, width), F32),
            scratch((width, width), F32),
        ]
        + [scratch(item.shape, BF16) for item in big]
        + [scratch((edges, width), BF16)] * 2
        + [scratch(near_shape, BF16), scratch(far_shape, BF16)] * 3
        + [scratch(item, BF16) for item in grad_shapes]
        + [
            scratch((2,) * (bits - 1 - phase) + (s, width), BF16)
            for s in slabs
            for phase in range(bits)
        ]
        + [
            scratch((2,) * (bits - 1 - phase) + (s, width), BF16)
            for s in slabs
            for phase in range(bits - 1)
        ]
        + [dma((4, bits)), dma((4, bits)), dma((6,)), dma((2,))]
        + swap_sems(peers)
        + swap_sems(peers),
        compiler_params=pltpu.CompilerParams(
            collective_id=2, has_side_effects=True, vmem_limit_bytes=67043328
        ),
        cost_estimate=pl.CostEstimate(flops=10**10, bytes_accessed=10**8, transcendentals=0),
    )(
        owner,
        node,
        ncot,
        code.reshape(edges // tile, 1, tile),
        recv_at.reshape(edges // tile, 1, tile),
        *big,
    )


def close_kernel(count, owner_ref, part_ref, near_ref, far_ref, *refs):
    refs = list(refs)
    sums = refs[:4]
    passed = refs[4 : 4 + count]
    grad_ref = refs[4 + count]
    targets = refs[5 + count : 9 + count]
    passed_out = refs[9 + count : 9 + 2 * count]
    held = refs[9 + 2 * count : 9 + 3 * count]
    sem = refs[-1]
    into = [
        pltpu.make_async_copy(a, b, sem.at[0, k]) for k, (a, b) in enumerate(zip(passed, held))
    ]
    out = [
        pltpu.make_async_copy(a, b, sem.at[1, k])
        for k, (a, b) in enumerate(zip(held, passed_out))
    ]
    for copy in into:
        copy.start()
    nodes = part_ref.shape[0]
    near = near_ref.shape[0]
    hot = col_hot(owner_ref[...], nodes)
    total = part_ref[...] + dot(hot[:, :near], near_ref[...])
    grad_ref[...] = (total + dot(hot[:, near:], far_ref[...])).astype(BF16)
    for source, target in zip(sums, targets):
        target[...] = source[...]
    for one, two in zip(into, out):
        one.wait()
        two.start()
    for copy in out:
        copy.wait()


def close(owner, part, near, far, sums, passed):
    vmem = pl.BlockSpec(memory_space=pltpu.VMEM)
    anywhere = pl.BlockSpec(memory_space=pl.ANY)
    count = len(passed)
    shape = jax.ShapeDtypeStruct
    return pl.pallas_call(
        functools.partial(close_kernel, count),
        name="close",
        out_shape=(shape(part.shape, BF16),)
        + tuple(shape(item.shape, F32) for item in sums)
        + tuple(shape(item.shape, BF16) for item in passed),
        in_specs=[vmem] * 8 + [anywhere] * count,
        out_specs=[vmem] * 5 + [anywhere] * count,
        scratch_shapes=[pltpu.VMEM(item.shape, BF16) for item in passed]
        + [pltpu.SemaphoreType.DMA((2, count))],
        compiler_params=pltpu.CompilerParams(vmem_limit_bytes=67043328),
    )(owner, part, near, far, *sums, *passed)


def shards(
    node_latent,
    edge_latent,
    node_cotangent,
    edge_cotangent,
    w_edge_in,
    w_edge_out,
    w_node_in,
    w_node_out,
    sender_code,
    receiver,
    near_list,
    far_list,
):
    node_rows, width = node_latent.shape
    edge_rows = edge_latent.shape[0]
    peers = lax.axis_size("row") * lax.axis_size("col")
    near_shape = (4, near_list.shape[2], width)
    far_shape = (peers, far_list.shape[2], width)
    owner = jnp.concatenate([near_list.reshape(-1), far_list.reshape(-1)], 0)[None, :]
    scales = (1.0 / math.sqrt(edge_rows * peers), 1.0 / math.sqrt(node_rows * peers))
    big = (edge_latent, edge_cotangent, w_edge_in, w_edge_out, w_node_in, w_node_out)
    if all(item.shape[0] % (16 * peers) == 0 for item in big[2:]):
        node_new, edge_new, grad_edge, part, near_back, far_back, *sums = whole(
            owner,
            node_latent,
            node_cotangent,
            sender_code,
            receiver,
            big,
            near_shape,
            far_shape,
            scales,
        )
        grad_node, s_in, s_hin, s_out, s_hout, node_new, edge_new, grad_edge = close(
            owner,
            part,
            near_back.reshape(-1, width),
            far_back.reshape(-1, width),
            sums,
            (node_new, edge_new, grad_edge),
        )
        return (node_new, edge_new, grad_node, grad_edge, s_in, s_out, s_hin, s_hout)
    near, far = halo(owner, node_latent, near_shape, far_shape)
    node_new, edge_new, part, grad_edge, near_grad, far_grad, g_in, g_out, h_in, h_out = compute(
        node_latent,
        edge_latent,
        node_cotangent,
        edge_cotangent,
        w_edge_in,
        w_edge_out,
        w_node_in,
        w_node_out,
        sender_code,
        receiver,
        near.reshape(-1, width),
        far.reshape(-1, width),
        scales,
    )
    *sums, near_back, far_back = scatter_sum(
        (g_in, h_in, g_out, h_out), near_grad.reshape(near_shape), far_grad.reshape(far_shape)
    )
    grad_node, s_in, s_hin, s_out, s_hout = finish(
        owner, part, near_back.reshape(-1, width), far_back.reshape(-1, width), sums
    )
    return (node_new, edge_new, grad_node, grad_edge, s_in, s_out, s_hin, s_hout)


def solution(mesh):
    both = ("row", "col")
    in_specs = (
        P(both, None),
        P(both, None),
        P(both, None),
        P(both, None),
        P(),
        P(),
        P(),
        P(),
        P(both),
        P(both),
        P(both, None, None),
        P(both, None, None),
    )
    out_specs = (P(both, None),) * 8
    return jax.shard_map(shards, mesh=mesh, in_specs=in_specs, out_specs=out_specs, check_vma=False)
```

```python
import functools
import math

import jax
import jax.numpy as jnp
from jax import lax
from jax.experimental import pallas as pl
from jax.experimental.pallas import tpu as pltpu
from jax.sharding import PartitionSpec as P

EPS = 1e-05
MESH = pl.DeviceIdType.MESH
F32 = jnp.float32
BF16 = jnp.bfloat16


def dot(left, right):
    return jnp.dot(left, right, preferred_element_type=F32)


def dot_t(left, weight):
    return lax.dot_general(left, weight, (((1,), (1,)), ((), ())), preferred_element_type=F32)


def cross(left, right):
    return lax.dot_general(left, right, (((0,), (0,)), ((), ())), preferred_element_type=F32)


def norm_parts(value):
    mean = jnp.mean(value, -1, keepdims=True)
    centred = value - mean
    recip = lax.rsqrt(jnp.mean(centred * centred, -1, keepdims=True) + EPS)
    return centred * recip, recip


def norm_back(normed, recip, grad):
    inner = (
        grad
        - jnp.mean(grad, -1, keepdims=True)
        - normed * jnp.mean(grad * normed, -1, keepdims=True)
    )
    return recip * inner


def row_hot(codes, count):
    tile = codes.shape[1]
    column = jnp.transpose(jnp.broadcast_to(codes, (128, tile)))
    lane = lax.broadcasted_iota(jnp.int32, (tile, 128), 1)
    groups = [
        jnp.where(column == lane + 128 * g, 1.0, 0.0).astype(BF16) for g in range(count // 128)
    ]
    return jnp.concatenate(groups, 1)


def col_hot(codes, count):
    tile = codes.shape[1]
    ids = lax.broadcasted_iota(jnp.int32, (count, tile), 0)
    return jnp.where(codes == ids, 1.0, 0.0).astype(BF16)


def flat(lists):
    high, low = lists.shape
    count = high * low
    spread = lax.broadcasted_iota(jnp.int32, (low, count), 1) % low
    spread = jnp.where(spread == lax.broadcasted_iota(jnp.int32, (low, count), 0), 1.0, 0.0)
    wide = jnp.dot(
        lists.astype(F32), spread, precision=lax.Precision.HIGHEST, preferred_element_type=F32
    )
    keep = lax.broadcasted_iota(jnp.int32, (high, count), 1) // low
    keep = keep == lax.broadcasted_iota(jnp.int32, (high, count), 0)
    return jnp.sum(jnp.where(keep, wide, 0.0), 0, keepdims=True).astype(jnp.int32)


def compute_kernel(
    tile,
    edge_scale,
    node_scale,
    node_ref,
    edge_ref,
    ncot_ref,
    ecot_ref,
    w_in,
    w_out,
    v_in,
    v_out,
    code_ref,
    recv_ref,
    near_ref,
    far_ref,
    node_new_ref,
    edge_new_ref,
    part_ref,
    grad_edge_ref,
    near_grad_ref,
    far_grad_ref,
    g_in_ref,
    g_out_ref,
    h_in_ref,
    h_out_ref,
    proj,
    slope,
    normed_s,
    recip_s,
    hidden_s,
    gath_s,
    gg_s,
    sums_s,
    acc_e,
    acc_o,
):
    nodes, width = node_ref.shape
    edges = edge_ref.shape[0]
    near = near_ref.shape[0]
    far = far_ref.shape[0]
    rows = nodes + near + far
    steps = edges // tile
    w_e = w_in.at[pl.ds(0, width)]
    w_s = w_in.at[pl.ds(width, width)]
    w_r = w_in.at[pl.ds(2 * width, width)]
    v_a = v_in.at[pl.ds(0, width)]
    v_b = v_in.at[pl.ds(width, width)]
    proj[pl.ds(0, nodes), :] = dot(node_ref[...], w_s[...]).astype(BF16)
    proj[pl.ds(nodes, near), :] = dot(near_ref[...], w_s[...]).astype(BF16)
    proj[pl.ds(nodes + near, far), :] = dot(far_ref[...], w_s[...]).astype(BF16)
    proj[pl.ds(rows, nodes), :] = dot(node_ref[...], w_r[...]).astype(BF16)
    gath_s[...] = jnp.zeros_like(gath_s)

    def forward(step, carry):
        span = pl.ds(pl.multiple_of(step * tile, tile), tile)
        codes = code_ref[step]
        recvs = recv_ref[step]
        hot = jnp.concatenate([row_hot(codes, rows), row_hot(recvs, nodes)], 1)
        edge = edge_ref[span, :]
        pre = dot(edge, w_e[...]) + dot(hot, proj[...])
        sigma = jax.nn.sigmoid(pre)
        slope[span, :] = sigma * (1.0 + pre * (1.0 - sigma))
        hidden = (pre * sigma).astype(BF16)
        hidden_s[span, :] = hidden
        normed, recip = norm_parts(dot(hidden, w_out[...]))
        normed_s[span, :] = normed
        recip_s[span, :] = jnp.broadcast_to(recip, (tile, 128))
        new = (edge.astype(F32) + normed).astype(BF16)
        edge_new_ref[span, :] = new
        gath_s[...] += dot(col_hot(recvs, nodes), new)
        return carry

    lax.fori_loop(0, steps, forward, 0)

    node = node_ref[...]
    gathered = gath_s[...].astype(BF16)
    pre = dot(node, v_a[...]) + dot(gathered, v_b[...])
    sigma = jax.nn.sigmoid(pre)
    hidden = (pre * sigma).astype(BF16)
    normed, recip = norm_parts(dot(hidden, v_out[...]))
    node_new_ref[...] = (node.astype(F32) + normed).astype(BF16)
    ncot = ncot_ref[...].astype(F32)
    delta = norm_back(normed, recip, ncot).astype(BF16)
    pre_delta = (dot_t(delta, v_out[...]) * (sigma * (1.0 + pre * (1.0 - sigma)))).astype(BF16)
    gg_s[...] = dot_t(pre_delta, v_b[...]).astype(BF16)
    part_ref[...] = ncot + dot_t(pre_delta, v_a[...])
    h_in_ref[pl.ds(0, width), :] = (cross(node, pre_delta) * node_scale).astype(BF16)
    h_in_ref[pl.ds(width, width), :] = (cross(gathered, pre_delta) * node_scale).astype(BF16)
    h_out_ref[...] = (cross(hidden, delta) * node_scale).astype(BF16)

    sums_s[...] = jnp.zeros_like(sums_s)
    acc_e[...] = jnp.zeros_like(acc_e)
    acc_o[...] = jnp.zeros_like(acc_o)

    def backward(step, carry):
        span = pl.ds(pl.multiple_of(step * tile, tile), tile)
        codes = code_ref[step]
        recvs = recv_ref[step]
        total = ecot_ref[span, :].astype(F32) + dot(row_hot(recvs, nodes), gg_s[...])
        recip = recip_s[span, :][:, :1]
        delta = norm_back(normed_s[span, :], recip, total).astype(BF16)
        pre_delta = (dot_t(delta, w_out[...]) * slope[span, :]).astype(BF16)
        grad_edge_ref[span, :] = (total + dot_t(pre_delta, w_e[...])).astype(BF16)
        hot = jnp.concatenate([col_hot(codes, rows), col_hot(recvs, nodes)], 0)
        sums_s[...] += dot(hot, pre_delta)
        acc_e[...] += cross(edge_ref[span, :], pre_delta)
        acc_o[...] += cross(hidden_s[span, :], delta)
        return carry

    lax.fori_loop(0, steps, backward, 0)

    g_in_ref[pl.ds(0, width), :] = (acc_e[...] * edge_scale).astype(BF16)
    g_out_ref[...] = (acc_o[...] * edge_scale).astype(BF16)
    own_sum = sums_s[pl.ds(0, nodes), :].astype(BF16)
    near_sum = sums_s[pl.ds(nodes, near), :].astype(BF16)
    far_sum = sums_s[pl.ds(nodes + near, far), :].astype(BF16)
    recv_sum = sums_s[pl.ds(rows, nodes), :].astype(BF16)
    near_grad_ref[...] = dot_t(near_sum, w_s[...]).astype(BF16)
    far_grad_ref[...] = dot_t(far_sum, w_s[...]).astype(BF16)
    part_ref[...] += dot_t(own_sum, w_s[...]) + dot_t(recv_sum, w_r[...])
    sent = cross(node_ref[...], own_sum) + cross(near_ref[...], near_sum)
    sent += cross(far_ref[...], far_sum)
    g_in_ref[pl.ds(width, width), :] = (sent * edge_scale).astype(BF16)
    g_in_ref[pl.ds(2 * width, width), :] = (cross(node_ref[...], recv_sum) * edge_scale).astype(BF16)


def compute(node, edge, ncot, ecot, w_in, w_out, v_in, v_out, code, recv, near, far, scales):
    nodes, width = node.shape
    edges = edge.shape[0]
    rows = nodes + near.shape[0] + far.shape[0]
    tile = math.gcd(edges, 512)
    vmem = pl.BlockSpec(memory_space=pltpu.VMEM)
    shape = jax.ShapeDtypeStruct
    units = 2 * edges * width
    work = units * width * 5 + units * (2 * (rows + nodes) + 2 * nodes)
    return pl.pallas_call(
        functools.partial(compute_kernel, tile, *scales),
        name="processor",
        out_shape=(
            shape((nodes, width), BF16),
            shape((edges, width), BF16),
            shape((nodes, width), F32),
            shape((edges, width), BF16),
            shape(near.shape, BF16),
            shape(far.shape, BF16),
            shape(w_in.shape, BF16),
            shape(w_out.shape, BF16),
            shape(v_in.shape, BF16),
            shape(v_out.shape, BF16),
        ),
        in_specs=[vmem] * 12,
        out_specs=[vmem] * 10,
        scratch_shapes=[
            pltpu.VMEM((rows + nodes, width), BF16),
            pltpu.VMEM((edges, width), F32),
            pltpu.VMEM((edges, width), F32),
            pltpu.VMEM((edges, 128), F32),
            pltpu.VMEM((edges, width), BF16),
            pltpu.VMEM((nodes, width), F32),
            pltpu.VMEM((nodes, width), BF16),
            pltpu.VMEM((rows + nodes, width), F32),
            pltpu.VMEM((width, width), F32),
            pltpu.VMEM((width, width), F32),
        ],
        compiler_params=pltpu.CompilerParams(vmem_limit_bytes=62 * 1024 * 1024),
        cost_estimate=pl.CostEstimate(flops=work, bytes_accessed=20 * units, transcendentals=units),
    )(
        node,
        edge,
        ncot,
        ecot,
        w_in,
        w_out,
        v_in,
        v_out,
        code.reshape(edges // tile, 1, tile),
        recv.reshape(edges // tile, 1, tile),
        near,
        far,
    )


def bit_count(size):
    bits = size.bit_length() - 1
    assert size == 1 << bits
    return bits


class Swap:
    def __init__(self, sign, near_src, far_src, near_dst, far_dst, sems):
        self.row = lax.axis_index("row")
        self.col = lax.axis_index("col")
        self.rows = lax.axis_size("row")
        self.cols = lax.axis_size("col")
        self.peers = self.rows * self.cols
        self.me = self.row * self.cols + self.col
        self.sign = sign
        self.near = (near_src, near_dst)
        self.far = (far_src, far_dst)
        self.near_send, self.near_recv, self.far_send, self.far_recv, self.own = sems

    def place(self, peer):
        return (peer // self.cols, peer % self.cols)

    def greet(self):
        barrier = pltpu.get_barrier_semaphore()

        def signal(k, carry):
            peer = self.place((self.me + k) % self.peers)
            pl.semaphore_signal(barrier, inc=1, device_id=peer, device_id_type=MESH)
            return carry

        lax.fori_loop(1, self.peers, signal, 0)
        pl.semaphore_wait(barrier, self.peers - 1)

    def near_copy(self, k):
        by = self.sign * (1, -1, 1, -1)[k]
        row, col = self.row, self.col
        if k < 2:
            row = (row + by + self.rows) % self.rows
        else:
            col = (col + by + self.cols) % self.cols
        return pltpu.make_async_remote_copy(
            src_ref=self.near[0].at[k],
            dst_ref=self.near[1].at[k],
            send_sem=self.near_send.at[k],
            recv_sem=self.near_recv.at[k],
            device_id=(row, col),
            device_id_type=MESH,
        )

    def far_copy(self, k):
        peer = (self.me + k) % self.peers
        return pltpu.make_async_remote_copy(
            src_ref=self.far[0].at[peer],
            dst_ref=self.far[1].at[self.me],
            send_sem=self.far_send.at[k],
            recv_sem=self.far_recv.at[k],
            device_id=self.place(peer),
            device_id_type=MESH,
        )

    def own_copy(self):
        return pltpu.make_async_copy(
            self.far[0].at[self.me], self.far[1].at[self.me], self.own.at[0]
        )

    def start(self):
        for k in range(4):
            self.near_copy(k).start()

        def begin(k, carry):
            self.far_copy(k).start()
            return carry

        lax.fori_loop(1, self.peers, begin, 0)
        self.own_copy().start()

    def wait(self):
        for k in range(4):
            self.near_copy(k).wait()

        def end(k, carry):
            self.far_copy(k).wait()
            return carry

        lax.fori_loop(1, self.peers, end, 0)
        self.own_copy().wait()


def swap_sems(peers):
    dma = pltpu.SemaphoreType.DMA
    return [dma((4,)), dma((4,)), dma((peers,)), dma((peers,)), dma((1,))]


def halo_kernel(owner_ref, node_ref, near_ref, far_ref, near_s, far_s, *sems):
    nodes = node_ref.shape[0]
    near_rows = near_s.shape[0] * near_s.shape[1]
    swap = Swap(1, near_s, far_s, near_ref, far_ref, sems)
    offered = cross(col_hot(owner_ref[...], nodes), node_ref[...])
    near_s[...] = offered[:near_rows].reshape(near_s.shape).astype(BF16)
    far_s[...] = offered[near_rows:].reshape(far_s.shape).astype(BF16)
    swap.greet()
    swap.start()
    swap.wait()


def halo(owner, node, near_shape, far_shape):
    vmem = pl.BlockSpec(memory_space=pltpu.VMEM)
    return pl.pallas_call(
        halo_kernel,
        name="halo",
        out_shape=(
            jax.ShapeDtypeStruct(near_shape, BF16),
            jax.ShapeDtypeStruct(far_shape, BF16),
        ),
        in_specs=[vmem] * 2,
        out_specs=[vmem] * 2,
        scratch_shapes=[pltpu.VMEM(near_shape, BF16), pltpu.VMEM(far_shape, BF16)]
        + swap_sems(far_shape[0]),
        compiler_params=pltpu.CompilerParams(collective_id=1, has_side_effects=True),
        cost_estimate=pl.CostEstimate(flops=10**8, bytes_accessed=10**7, transcendentals=0),
    )(owner, node)


def scatter_kernel(orders, row_bits, col_bits, count, *refs):
    bits = row_bits + col_bits
    refs = list(refs)

    def taken(number):
        got = refs[:number]
        del refs[:number]
        return got

    inputs = taken(count)
    near_src, far_src = taken(2)
    outputs = taken(count)
    near_dst, far_dst = taken(2)
    recv = [taken(bits) for _ in range(count)]
    held = [taken(bits) for _ in range(count)]
    send_sem, recv_sem, local_sem = taken(3)
    row = lax.axis_index("row")
    col = lax.axis_index("col")
    swap = Swap(-1, near_src, far_src, near_dst, far_dst, refs)

    def mine(bit):
        if bit < row_bits:
            return (row // (1 << (row_bits - 1 - bit))) % 2
        return (col // (1 << (bits - 1 - bit))) % 2

    def partner(bit):
        if bit < row_bits:
            step = 1 << (row_bits - 1 - bit)
            return (row + step * (1 - 2 * mine(bit)), col)
        step = 1 << (bits - 1 - bit)
        return (row, col + step * (1 - 2 * mine(bit)))

    swap.greet()
    left = [list(range(bits)) for _ in range(count)]
    current = list(inputs)

    def copy_of(a, phase):
        bit = orders[a][phase]
        place = left[a].index(bit)
        spot = (slice(None),) * place + (1 - mine(bit),)
        return pltpu.make_async_remote_copy(
            src_ref=current[a].at[spot],
            dst_ref=recv[a][phase],
            send_sem=send_sem.at[a, phase],
            recv_sem=recv_sem.at[a, phase],
            device_id=partner(bit),
            device_id_type=MESH,
        )

    copies = [copy_of(a, 0) for a in range(count)]
    for item in copies:
        item.start()
    swap.start()
    kept = []
    for a in range(count):
        bit = orders[a][0]
        place = left[a].index(bit)
        spot = (slice(None),) * place + (mine(bit),)
        kept.append(pltpu.make_async_copy(inputs[a].at[spot], held[a][0], local_sem.at[a]))
        kept[a].start()
    sent = []
    for phase in range(bits):
        for a in range(count):
            copies[a].wait_recv()
            sent.append(copies[a])
            bit = orders[a][phase]
            place = left[a].index(bit)
            spot = (slice(None),) * place + (mine(bit),)
            left[a].remove(bit)
            if phase == 0:
                kept[a].wait()
                own = held[a][0][...]
            else:
                own = current[a][spot]
            value = own.astype(F32) + recv[a][phase][...].astype(F32)
            if phase == bits - 1:
                outputs[a][...] = value
            else:
                current[a] = held[a][phase]
                current[a][...] = value.astype(BF16)
                copies[a] = copy_of(a, phase + 1)
                copies[a].start()
    for item in sent:
        item.wait_send()
    swap.wait()


def scatter_sum(grads, near_grad, far_grad):
    rows_grid = lax.axis_size("row")
    cols_grid = lax.axis_size("col")
    row_bits = bit_count(rows_grid)
    col_bits = bit_count(cols_grid)
    bits = row_bits + col_bits
    peers = rows_grid * cols_grid
    width = grads[0].shape[-1]
    slabs = [g.shape[0] // peers for g in grads]
    shaped = [g.reshape((2,) * bits + (s, width)) for g, s in zip(grads, slabs)]
    core = bits - 1
    along_col = list(range(bits - 2, row_bits - 1, -1))
    row_near = [row_bits - 1]
    row_far = list(range(row_bits - 2, -1, -1))
    turns = [
        [core] + along_col + row_near + row_far,
        [core] + row_near + row_far + along_col,
        [core] + row_far + along_col + row_near,
        [core] + row_far + along_col + row_near,
    ]
    count = len(grads)
    vmem = pl.BlockSpec(memory_space=pltpu.VMEM)
    anywhere = pl.BlockSpec(memory_space=pl.ANY)
    recv = [
        pltpu.VMEM((2,) * (bits - 1 - phase) + (s, width), BF16)
        for s in slabs
        for phase in range(bits)
    ]
    shape = jax.ShapeDtypeStruct
    dma = pltpu.SemaphoreType.DMA
    return pl.pallas_call(
        functools.partial(scatter_kernel, turns, row_bits, col_bits, count),
        name="scatter_sum",
        out_shape=tuple(shape((s, width), F32) for s in slabs)
        + (shape(near_grad.shape, BF16), shape(far_grad.shape, BF16)),
        in_specs=[anywhere] * count + [vmem] * 2,
        out_specs=[vmem] * (count + 2),
        scratch_shapes=recv
        + recv
        + [dma((count, bits)), dma((count, bits)), dma((count,))]
        + swap_sems(peers),
        compiler_params=pltpu.CompilerParams(
            collective_id=0, has_side_effects=True, vmem_limit_bytes=40 * 1024 * 1024
        ),
        cost_estimate=pl.CostEstimate(flops=10**9, bytes_accessed=10**8, transcendentals=0),
    )(*shaped, near_grad, far_grad)


def finish_kernel(count, owner_ref, part_ref, near_ref, far_ref, *refs):
    nodes = part_ref.shape[0]
    near = near_ref.shape[0]
    sums = refs[:count]
    grad_ref = refs[count]
    hot = col_hot(owner_ref[...], nodes)
    total = part_ref[...] + dot(hot[:, :near], near_ref[...])
    grad_ref[...] = (total + dot(hot[:, near:], far_ref[...])).astype(BF16)
    for source, target in zip(sums, refs[count + 1 :]):
        target[...] = source[...]


def finish(owner, part, near, far, sums):
    vmem = pl.BlockSpec(memory_space=pltpu.VMEM)
    count = len(sums)
    return pl.pallas_call(
        functools.partial(finish_kernel, count),
        name="finish",
        out_shape=(jax.ShapeDtypeStruct(part.shape, BF16),)
        + tuple(jax.ShapeDtypeStruct(item.shape, F32) for item in sums),
        in_specs=[vmem] * (4 + count),
        out_specs=[vmem] * (1 + count),
    )(owner, part, near, far, *sums)


class Halving:
    def __init__(self, order, row_bits, col_bits, source, recv, held, out, send_sem, recv_sem, at):
        self.order = order
        self.row_bits = row_bits
        self.bits = row_bits + col_bits
        self.left = list(range(self.bits))
        self.current = source
        self.recv, self.held, self.out = recv, held, out
        self.send_sem, self.recv_sem = send_sem, recv_sem
        self.at = at
        self.sent = []
        self.phase = 0

    def mine(self, bit):
        if bit < self.row_bits:
            return (lax.axis_index("row") // (1 << (self.row_bits - 1 - bit))) % 2
        return (lax.axis_index("col") // (1 << (self.bits - 1 - bit))) % 2

    def partner(self, bit):
        row, col = lax.axis_index("row"), lax.axis_index("col")
        if bit < self.row_bits:
            return (row + (1 << (self.row_bits - 1 - bit)) * (1 - 2 * self.mine(bit)), col)
        return (row, col + (1 << (self.bits - 1 - bit)) * (1 - 2 * self.mine(bit)))

    def spot(self, bit, which):
        lead = [slice(None)] * len(self.left)
        lead[self.left.index(bit)] = which
        if self.phase == 0 and self.at is not None:
            lead.append(pl.ds(self.at, 16))
        return tuple(lead)

    def start(self):
        bit = self.order[self.phase]
        copy = pltpu.make_async_remote_copy(
            src_ref=self.current.at[self.spot(bit, 1 - self.mine(bit))],
            dst_ref=self.recv[self.phase],
            send_sem=self.send_sem.at[self.phase],
            recv_sem=self.recv_sem.at[self.phase],
            device_id=self.partner(bit),
            device_id_type=MESH,
        )
        copy.start()
        self.sent.append(copy)

    def step(self):
        bit = self.order[self.phase]
        self.sent[-1].wait_recv()
        own = self.current[self.spot(bit, self.mine(bit))]
        value = own.astype(F32) + self.recv[self.phase][...].astype(F32)
        self.left.remove(bit)
        self.phase += 1
        if self.phase == self.bits:
            if self.at is None:
                self.out[...] = value
            else:
                self.out[pl.ds(self.at, 16), :] = value
            return
        self.current = self.held[self.phase - 1]
        self.current[...] = value.astype(BF16)
        self.start()

    def end(self):
        for copy in self.sent:
            copy.wait_send()


def whole_kernel(tile, scales, pieces, turns, row_bits, col_bits, *refs):
    edge_scale, node_scale = scales
    bits = row_bits + col_bits
    refs = list(refs)

    def taken(number):
        got = refs[:number]
        del refs[:number]
        return got

    near_list, far_list, node_ref, ncot_ref, code_ref, recv_ref = taken(6)
    loads = taken(6)
    node_new_ref, edge_new_ref, grad_edge_ref, part_ref, near_back, far_back = taken(6)
    outputs = taken(4)
    proj, slope, normed_s, recip_s, hidden_s, gath_s, gg_s, sums_s, acc_e, acc_o = taken(10)
    held_in = taken(6)
    edge_new_s, grad_edge_s = taken(2)
    near_s, far_s, near_r, far_r, near_g, far_g = taken(6)
    grads = taken(4)
    recv = [taken(bits) for _ in pieces]
    held = [taken(bits - 1) for _ in pieces]
    send_sem, recv_sem, load_sem, store_sem = taken(4)
    out_swap = Swap(1, near_s, far_s, near_r, far_r, taken(5))
    back_swap = Swap(-1, near_g, far_g, near_back, far_back, taken(5))

    copies = []
    for k in (0, 2, 3, 4, 5, 1):
        copies.append(pltpu.make_async_copy(loads[k], held_in[k], load_sem.at[k]))
        copies[-1].start()
    edge_s, ecot_s, w_in, w_out, v_in, v_out = held_in
    edge_copy, w_in_copy, w_out_copy, v_in_copy, v_out_copy, ecot_copy = copies

    nodes, width = node_ref.shape
    edges = edge_s.shape[0]
    near = near_s.shape[0] * near_s.shape[1]
    far = far_s.shape[0] * far_s.shape[1]
    rows = nodes + near + far
    steps = edges // tile
    w_e = w_in.at[pl.ds(0, width)]
    w_s = w_in.at[pl.ds(width, width)]
    w_r = w_in.at[pl.ds(2 * width, width)]
    v_a = v_in.at[pl.ds(0, width)]
    v_b = v_in.at[pl.ds(width, width)]

    def span_of(step):
        if isinstance(step, int):
            return pl.ds(step * tile, tile)
        return pl.ds(pl.multiple_of(step * tile, tile), tile)

    offer = cross(col_hot(flat(near_list[...]), nodes), node_ref[...])
    near_s[...] = offer.reshape(near_s.shape).astype(BF16)
    offer = cross(col_hot(flat(far_list[...]), nodes), node_ref[...])
    far_s[...] = offer.reshape(far_s.shape).astype(BF16)
    out_swap.greet()
    out_swap.start()

    edge_copy.wait()
    w_in_copy.wait()
    gath_s[...] = jnp.zeros_like(gath_s)
    sums_s[...] = jnp.zeros_like(sums_s)
    acc_e[...] = jnp.zeros_like(acc_e)
    acc_o[...] = jnp.zeros_like(acc_o)
    proj[pl.ds(0, nodes), :] = dot(node_ref[...], w_s[...]).astype(BF16)
    proj[pl.ds(rows, nodes), :] = dot(node_ref[...], w_r[...]).astype(BF16)

    def ahead(step, carry):
        span = span_of(step)
        hot = row_hot(recv_ref[step], nodes)
        slope[span, :] = dot(edge_s[span, :], w_e[...]) + dot(hot, proj[pl.ds(rows, nodes), :])
        return carry

    lax.fori_loop(0, steps, ahead, 0)
    w_out_copy.wait()
    v_in_copy.wait()
    v_out_copy.wait()
    ecot_copy.wait()
    out_swap.wait()
    near_rows = near_r[...].astype(F32).reshape(near, width).astype(BF16)
    far_rows = far_r[...].astype(F32).reshape(far, width).astype(BF16)
    proj[pl.ds(nodes, near), :] = dot(near_rows, w_s[...]).astype(BF16)
    proj[pl.ds(nodes + near, far), :] = dot(far_rows, w_s[...]).astype(BF16)

    def forward(step, carry):
        span = span_of(step)
        edge = edge_s[span, :]
        pre = slope[span, :] + dot(row_hot(code_ref[step], rows), proj[pl.ds(0, rows), :])
        sigma = jax.nn.sigmoid(pre)
        slope[span, :] = sigma * (1.0 + pre * (1.0 - sigma))
        hidden = (pre * sigma).astype(BF16)
        hidden_s[span, :] = hidden
        normed, recip = norm_parts(dot(hidden, w_out[...]))
        normed_s[span, :] = normed
        recip_s[span, :] = jnp.broadcast_to(recip, (tile, 128))
        new = (edge.astype(F32) + normed).astype(BF16)
        edge_new_s[span, :] = new
        gath_s[...] += dot(col_hot(recv_ref[step], nodes), new)
        return carry

    lax.fori_loop(0, steps, forward, 0)
    edge_new_copy = pltpu.make_async_copy(edge_new_s, edge_new_ref, store_sem.at[0])
    edge_new_copy.start()

    node = node_ref[...]
    gathered = gath_s[...].astype(BF16)
    pre = dot(node, v_a[...]) + dot(gathered, v_b[...])
    sigma = jax.nn.sigmoid(pre)
    hidden = (pre * sigma).astype(BF16)
    normed, recip = norm_parts(dot(hidden, v_out[...]))
    node_new_ref[...] = (node.astype(F32) + normed).astype(BF16)
    ncot = ncot_ref[...].astype(F32)
    delta = norm_back(normed, recip, ncot).astype(BF16)
    pre_delta = (dot_t(delta, v_out[...]) * (sigma * (1.0 + pre * (1.0 - sigma)))).astype(BF16)
    g_in, h_in, g_out, h_out = grads
    h_in[pl.ds(0, width), :] = (cross(node, pre_delta) * node_scale).astype(BF16)
    h_in[pl.ds(width, width), :] = (cross(gathered, pre_delta) * node_scale).astype(BF16)
    h_out[...] = (cross(hidden, delta) * node_scale).astype(BF16)

    halvings = []
    for a in range(len(pieces)):
        which, at = pieces[a]
        slab = outputs[which].shape[0]
        source = grads[which].reshape((2,) * bits + (slab, width))
        halvings.append(
            Halving(
                turns[a],
                row_bits,
                col_bits,
                source,
                recv[a],
                held[a],
                outputs[which],
                send_sem.at[a],
                recv_sem.at[a],
                at if slab > 16 else None,
            )
        )
    from_edges = [item for item, (which, _) in zip(halvings, pieces) if which % 2 == 0]
    from_nodes = [item for item, (which, _) in zip(halvings, pieces) if which % 2 == 1]
    for item in from_nodes:
        item.start()
    gg_s[...] = dot_t(pre_delta, v_b[...]).astype(BF16)
    part_ref[...] = ncot + dot_t(pre_delta, v_a[...])

    def backward(step, carry):
        span = span_of(step)
        recvs = recv_ref[step]
        total = ecot_s[span, :].astype(F32) + dot(row_hot(recvs, nodes), gg_s[...])
        recip = recip_s[span, :][:, :1]
        delta = norm_back(normed_s[span, :], recip, total).astype(BF16)
        normed_s[span, :] = total
        pre_delta = (dot_t(delta, w_out[...]) * slope[span, :]).astype(BF16)
        acc_o[...] += cross(hidden_s[span, :], delta)
        hidden_s[span, :] = pre_delta
        sums_s[pl.ds(0, rows), :] += dot(col_hot(code_ref[step], rows), pre_delta)
        sums_s[pl.ds(rows, nodes), :] += dot(col_hot(recvs, nodes), pre_delta)
        acc_e[...] += cross(edge_s[span, :], pre_delta)
        return carry

    if steps <= 4:
        for k in range(steps):
            backward(k, 0)
            for item in from_nodes:
                item.step()
    else:
        lax.fori_loop(0, steps, backward, 0)
    g_in[pl.ds(0, width), :] = (acc_e[...] * edge_scale).astype(BF16)
    g_out[...] = (acc_o[...] * edge_scale).astype(BF16)
    own_sum = sums_s[pl.ds(0, nodes), :].astype(BF16)
    near_sum = sums_s[pl.ds(nodes, near), :].astype(BF16)
    far_sum = sums_s[pl.ds(nodes + near, far), :].astype(BF16)
    recv_sum = sums_s[pl.ds(rows, nodes), :].astype(BF16)
    sent = cross(node, own_sum) + cross(near_rows, near_sum) + cross(far_rows, far_sum)
    g_in[pl.ds(width, width), :] = (sent * edge_scale).astype(BF16)
    g_in[pl.ds(2 * width, width), :] = (cross(node, recv_sum) * edge_scale).astype(BF16)
    for item in from_edges:
        item.start()
    near_g[...] = dot_t(near_sum, w_s[...]).reshape(near_g.shape).astype(BF16)
    far_g[...] = dot_t(far_sum, w_s[...]).reshape(far_g.shape).astype(BF16)
    back_swap.start()
    part_ref[...] += dot_t(own_sum, w_s[...]) + dot_t(recv_sum, w_r[...])

    def behind(step, carry):
        span = span_of(step)
        change = dot_t(hidden_s[span, :], w_e[...])
        grad_edge_s[span, :] = (normed_s[span, :] + change).astype(BF16)
        return carry

    lax.fori_loop(0, steps, behind, 0)
    grad_edge_copy = pltpu.make_async_copy(grad_edge_s, grad_edge_ref, store_sem.at[1])
    grad_edge_copy.start()
    for phase in range(bits):
        for item in halvings:
            if item.phase <= phase:
                item.step()
    for item in halvings:
        item.end()
    back_swap.wait()
    edge_new_copy.wait()
    grad_edge_copy.wait()


def whole(near_list, far_list, node, ncot, code, recv_at, big, near_shape, far_shape, scales):
    row_bits = bit_count(lax.axis_size("row"))
    col_bits = bit_count(lax.axis_size("col"))
    bits = row_bits + col_bits
    peers = 1 << bits
    nodes, width = node.shape
    edges = big[0].shape[0]
    rows = nodes + near_shape[0] * near_shape[1] + far_shape[0] * far_shape[1]
    tile = math.gcd(edges, 512)
    grad_shapes = [big[2].shape, big[4].shape, big[3].shape, big[5].shape]
    slabs = [item[0] // peers for item in grad_shapes]
    core = bits - 1
    along_col = list(range(bits - 2, row_bits - 1, -1))
    row_near = [row_bits - 1]
    row_far = list(range(row_bits - 2, -1, -1))
    pieces = [(a, at) for a in (1, 3, 0, 2) for at in range(0, slabs[a], 16)]
    cycle = [
        [core] + row_far + along_col + row_near,
        [core] + row_near + row_far + along_col,
        [core] + along_col + row_near + row_far,
    ]
    turns = [cycle[k % 3] for k in range(len(pieces))]
    vmem = pl.BlockSpec(memory_space=pltpu.VMEM)
    anywhere = pl.BlockSpec(memory_space=pl.ANY)
    shape = jax.ShapeDtypeStruct
    dma = pltpu.SemaphoreType.DMA
    scratch = pltpu.VMEM
    return pl.pallas_call(
        functools.partial(whole_kernel, tile, scales, pieces, turns, row_bits, col_bits),
        name="whole_step",
        out_shape=(
            shape((nodes, width), BF16),
            shape((edges, width), BF16),
            shape((edges, width), BF16),
            shape((nodes, width), F32),
            shape(near_shape, BF16),
            shape(far_shape, BF16),
        )
        + tuple(shape((s, width), F32) for s in slabs),
        in_specs=[vmem] * 6 + [anywhere] * 6,
        out_specs=[vmem, anywhere, anywhere] + [vmem] * 7,
        scratch_shapes=[
            scratch((rows + nodes, width), BF16),
            scratch((edges, width), F32),
            scratch((edges, width), F32),
            scratch((edges, 128), F32),
            scratch((edges, width), BF16),
            scratch((nodes, width), F32),
            scratch((nodes, width), BF16),
            scratch((rows + nodes, width), F32),
            scratch((width, width), F32),
            scratch((width, width), F32),
        ]
        + [scratch(item.shape, BF16) for item in big]
        + [scratch((edges, width), BF16)] * 2
        + [scratch(near_shape, BF16), scratch(far_shape, BF16)] * 3
        + [scratch(item, BF16) for item in grad_shapes]
        + [
            scratch((2,) * (bits - 1 - phase) + (16, width), BF16)
            for _ in pieces
            for phase in range(bits)
        ]
        + [
            scratch((2,) * (bits - 1 - phase) + (16, width), BF16)
            for _ in pieces
            for phase in range(bits - 1)
        ]
        + [dma((len(pieces), bits)), dma((len(pieces), bits)), dma((6,)), dma((2,))]
        + swap_sems(peers)
        + swap_sems(peers),
        compiler_params=pltpu.CompilerParams(
            collective_id=2, has_side_effects=True, vmem_limit_bytes=67043328
        ),
        cost_estimate=pl.CostEstimate(flops=10**10, bytes_accessed=10**8, transcendentals=0),
    )(
        near_list,
        far_list,
        node,
        ncot,
        code.reshape(edges // tile, 1, tile),
        recv_at.reshape(edges // tile, 1, tile),
        *big,
    )


def close_kernel(count, near_list, far_list, part_ref, near_ref, far_ref, *refs):
    refs = list(refs)
    sums = refs[:4]
    passed = refs[4 : 4 + count]
    grad_ref = refs[4 + count]
    targets = refs[5 + count : 9 + count]
    passed_out = refs[9 + count : 9 + 2 * count]
    held = refs[9 + 2 * count : 9 + 3 * count]
    sem = refs[-1]
    into = [
        pltpu.make_async_copy(a, b, sem.at[0, k]) for k, (a, b) in enumerate(zip(passed, held))
    ]
    out = [
        pltpu.make_async_copy(a, b, sem.at[1, k])
        for k, (a, b) in enumerate(zip(held, passed_out))
    ]
    for copy in into:
        copy.start()
    nodes = part_ref.shape[0]
    total = part_ref[...] + dot(col_hot(flat(near_list[...]), nodes), near_ref[...])
    total += dot(col_hot(flat(far_list[...]), nodes), far_ref[...])
    grad_ref[...] = total.astype(BF16)
    for source, target in zip(sums, targets):
        target[...] = source[...]
    for one, two in zip(into, out):
        one.wait()
        two.start()
    for copy in out:
        copy.wait()


def close(near_list, far_list, part, near, far, sums, passed):
    vmem = pl.BlockSpec(memory_space=pltpu.VMEM)
    anywhere = pl.BlockSpec(memory_space=pl.ANY)
    count = len(passed)
    shape = jax.ShapeDtypeStruct
    return pl.pallas_call(
        functools.partial(close_kernel, count),
        name="close",
        out_shape=(shape(part.shape, BF16),)
        + tuple(shape(item.shape, F32) for item in sums)
        + tuple(shape(item.shape, BF16) for item in passed),
        in_specs=[vmem] * 9 + [anywhere] * count,
        out_specs=[vmem] * 5 + [anywhere] * count,
        scratch_shapes=[pltpu.VMEM(item.shape, BF16) for item in passed]
        + [pltpu.SemaphoreType.DMA((2, count))],
        compiler_params=pltpu.CompilerParams(vmem_limit_bytes=67043328),
    )(near_list, far_list, part, near, far, *sums, *passed)


def shards(
    node_latent,
    edge_latent,
    node_cotangent,
    edge_cotangent,
    w_edge_in,
    w_edge_out,
    w_node_in,
    w_node_out,
    sender_code,
    receiver,
    near_list,
    far_list,
):
    node_rows, width = node_latent.shape
    edge_rows = edge_latent.shape[0]
    peers = lax.axis_size("row") * lax.axis_size("col")
    near_shape = (4, near_list.shape[2], width)
    far_shape = (peers, far_list.shape[2], width)
    scales = (1.0 / math.sqrt(edge_rows * peers), 1.0 / math.sqrt(node_rows * peers))
    big = (edge_latent, edge_cotangent, w_edge_in, w_edge_out, w_node_in, w_node_out)
    if all(item.shape[0] % (16 * peers) == 0 for item in big[2:]):
        node_new, edge_new, grad_edge, part, near_back, far_back, *sums = whole(
            near_list[0],
            far_list[0],
            node_latent,
            node_cotangent,
            sender_code,
            receiver,
            big,
            near_shape,
            far_shape,
            scales,
        )
        grad_node, s_in, s_hin, s_out, s_hout, node_new, edge_new, grad_edge = close(
            near_list[0],
            far_list[0],
            part,
            near_back.reshape(-1, width),
            far_back.reshape(-1, width),
            sums,
            (node_new, edge_new, grad_edge),
        )
        return (node_new, edge_new, grad_node, grad_edge, s_in, s_out, s_hin, s_hout)
    owner = jnp.concatenate([near_list.reshape(-1), far_list.reshape(-1)], 0)[None, :]
    near, far = halo(owner, node_latent, near_shape, far_shape)
    node_new, edge_new, part, grad_edge, near_grad, far_grad, g_in, g_out, h_in, h_out = compute(
        node_latent,
        edge_latent,
        node_cotangent,
        edge_cotangent,
        w_edge_in,
        w_edge_out,
        w_node_in,
        w_node_out,
        sender_code,
        receiver,
        near.reshape(-1, width),
        far.reshape(-1, width),
        scales,
    )
    *sums, near_back, far_back = scatter_sum(
        (g_in, h_in, g_out, h_out), near_grad.reshape(near_shape), far_grad.reshape(far_shape)
    )
    grad_node, s_in, s_hin, s_out, s_hout = finish(
        owner, part, near_back.reshape(-1, width), far_back.reshape(-1, width), sums
    )
    return (node_new, edge_new, grad_node, grad_edge, s_in, s_out, s_hin, s_hout)


def solution(mesh):
    both = ("row", "col")
    in_specs = (
        P(both, None),
        P(both, None),
        P(both, None),
        P(both, None),
        P(),
        P(),
        P(),
        P(),
        P(both),
        P(both),
        P(both, None, None),
        P(both, None, None),
    )
    out_specs = (P(both, None),) * 8
    return jax.shard_map(shards, mesh=mesh, in_specs=in_specs, out_specs=out_specs, check_vma=False)
```
